512 devices in a mesh: tok: 16 (over z), head: 8 (over x, core), vid: 4 (over y).
Axes of the slice: x: 4, y: 4, z: 16, core: 2. Of those that a mesh axis runs over, the one named last changes fastest.
Arguments:
- queries: bfloat16 [4, 3, 2048, 8, 256], P('vid', None, 'tok', 'head'), may hold values from -6 to 6
- keys: bfloat16 [4, 3, 2048, 8, 256], P('vid', None, 'tok', 'head'), may hold values from -6 to 6
- values: bfloat16 [4, 3, 2048, 8, 256], P('vid', None, 'tok', 'head'), may hold values from -6 to 6
- out_grad: bfloat16 [4, 3, 2048, 8, 256], P('vid', None, 'tok', 'head'), may hold values from -6 to 6
- fast_init: bfloat16 [8, 3, 256, 256], P('head'), may hold values from -0.375 to 0.375
- updates: bfloat16 [4, 2, 8, 3, 256, 256], P('vid', None, 'head'), may hold values from -4 to 4
Outputs:
- query_grad: bfloat16 [4, 3, 2048, 8, 256], P('vid', None, 'tok', 'head')
- key_grad: bfloat16 [4, 3, 2048, 8, 256], P('vid', None, 'tok', 'head')
- value_grad: bfloat16 [4, 3, 2048, 8, 256], P('vid', None, 'tok', 'head')
- init_grad: float32 [8, 3, 256, 256], P('head')
The draws below stay inside these ranges and needn't reach their ends.
All inputs are finite; a program needn't handle non-finite values.
Results may differ from the reference program's by a relative error of at most 0.0014.
Values sent between devices are 32-bit elements; how exact they have to be, the bound alone decides.
A program may use at most 64 MiB of HBM per device.

```python
import jax
import jax.numpy as jnp
from jax import lax

HD = 256
GROUPS = 3
HEADS = 8
VIDEOS = 4
GROUP = 2048


def steps_of(rng, dims, pieces, smallest, top_value):
    level = 1.0
    for axis_at, blocks in pieces:
        draws = jax.random.uniform(jax.random.fold_in(jax.random.fold_in(rng, 6), axis_at), (blocks,), jnp.float32, smallest / len(pieces), top_value / len(pieces))
        level = level * jnp.repeat(jnp.exp(draws), dims[axis_at] // blocks).reshape((-1,) + (1,) * (len(dims) - 1 - axis_at))
    return level


def normal_values(key, dims, deviation, bound, cuts=(), dtype=jnp.bfloat16):
    gain = steps_of(key, dims, cuts, -0.22, 0.18) if cuts else 1.0
    values = jax.random.normal(key, dims, jnp.float32) * deviation * gain
    return jnp.minimum(jnp.maximum(values, -bound), bound).astype(dtype)


def setup_inputs(seed: int = 0) -> dict:
    seeds = jax.random.split(jax.random.key(seed), 7)
    return {
        "queries": normal_values(seeds[0], (VIDEOS, GROUPS, GROUP, HEADS, HD), 1.0, 6.0, ((0, 4), (2, 16), (3, 8))),
        "keys": normal_values(seeds[1], (VIDEOS, GROUPS, GROUP, HEADS, HD), 1.0, 6.0, ((0, 4), (2, 16), (3, 8))),
        "values": normal_values(seeds[2], (VIDEOS, GROUPS, GROUP, HEADS, HD), 1.0, 6.0, ((0, 4), (2, 16), (3, 8))),
        "out_grad": normal_values(seeds[3], (VIDEOS, GROUPS, GROUP, HEADS, HD), 1.0, 6.0, ((0, 4), (2, 16), (3, 8))),
        "fast_init": normal_values(seeds[4], (HEADS, 3, HD, HD), HD ** -0.5, 0.375, ((0, 8),)),
        "updates": normal_values(seeds[5], (VIDEOS, GROUPS - 1, HEADS, 3, HD, HD), 0.5, 4.0, ((0, 4), (2, 8))),
    }


EPS = 1e-06
HIGH = lax.Precision.HIGHEST

def matmul(left, right):
    return jnp.dot(left, right, precision=HIGH, preferred_element_type=jnp.float32)

def swiglu(rows, weights):
    gate = matmul(rows, weights[0])
    upper = matmul(rows, weights[1])
    return matmul(jax.nn.silu(gate) * upper, weights[2])

def update(weights, key_rows, value_rows, scale):
    gate = matmul(key_rows, weights[0])
    upper = matmul(key_rows, weights[1])
    active = jax.nn.silu(gate)
    sigma = jax.nn.sigmoid(gate)
    down_step = matmul((active * upper).T, value_rows)
    back = matmul(value_rows, weights[2].T)
    gate_step = matmul(key_rows.T, back * upper * sigma * (1.0 + gate * (1.0 - sigma)))
    up_step = matmul(key_rows.T, back * active)
    return jnp.stack([gate_step, up_step, down_step]) * scale

def colnorm(weights, raised):
    old = jnp.sqrt(lax.optimization_barrier(jnp.sum(weights * weights, axis=-2)) + EPS)
    new = jnp.sqrt(lax.optimization_barrier(jnp.sum(raised * raised, axis=-2)) + EPS)
    return raised * (old / new)[..., None, :]

def one_pair(packed):
    init, steps, query, key_rows, value_rows, cot = packed
    scale = GROUP ** (-0.5)
    weights = [init]
    for index in range(GROUPS - 1):
        weights.append(colnorm(weights[index], weights[index] + steps[index]))
    adjoint = jnp.zeros_like(init)
    grads_q, grads_k, grads_v = ([], [], [])
    for index in reversed(range(GROUPS)):
        current = weights[index]
        if index + 1 < GROUPS:
            _, norm_back = jax.vjp(colnorm, current, current + steps[index])
            direct, upper_adj = norm_back(adjoint)
        else:
            direct = jnp.zeros_like(init)
            upper_adj = jnp.zeros_like(init)

        def local(wt, qq, kk, vv):
            return (swiglu(qq, wt), update(wt, kk, vv, scale))
        _, back = jax.vjp(local, current, query[index], key_rows[index], value_rows[index])
        wpart, dq, dk, dv = back((cot[index], upper_adj))
        adjoint = direct + upper_adj + wpart
        grads_q.append(dq)
        grads_k.append(dk)
        grads_v.append(dv)
    order = lambda items: jnp.stack(items[::-1])
    return (order(grads_q), order(grads_k), order(grads_v), adjoint)

def reference(queries, keys, values, out_grad, fast_init, updates):

    def arrange(array):
        moved = jnp.transpose(array.astype(jnp.float32), (0, 3, 1, 2, 4))
        return moved.reshape((VIDEOS * HEADS, GROUPS, GROUP, HD))
    init = jnp.broadcast_to(fast_init.astype(jnp.float32)[None], (VIDEOS, HEADS, 3, HD, HD))
    init = init.reshape((VIDEOS * HEADS, 3, HD, HD))
    steps = jnp.transpose(updates.astype(jnp.float32), (0, 2, 1, 3, 4, 5))
    steps = steps.reshape((VIDEOS * HEADS, GROUPS - 1, 3, HD, HD))
    dq, dk, dv, adjoint = lax.map(one_pair, (init, steps, arrange(queries), arrange(keys), arrange(values), arrange(out_grad)))

    def restore(array):
        shaped = array.reshape((VIDEOS, HEADS, GROUPS, GROUP, HD))
        return jnp.transpose(shaped, (0, 2, 3, 1, 4)).astype(jnp.bfloat16)
    init_grad = lax.optimization_barrier(jnp.sum(adjoint.reshape((VIDEOS, HEADS, 3, HD, HD)), axis=0))
    return (restore(dq), restore(dk), restore(dv), init_grad)
```

```python
import functools

import jax
import jax.numpy as jnp
from jax import lax
from jax.experimental import pallas as pl
from jax.experimental.pallas import tpu as pltpu
from jax.sharding import PartitionSpec as P

EPS = 1e-06
F32 = jnp.float32
BF16 = jnp.bfloat16
ROWS_PER_PIECE = 16


def nn(a, b):
    return lax.dot_general(a, b, (((1,), (0,)), ((), ())), preferred_element_type=F32)


def nt(a, b):
    return lax.dot_general(a, b, (((1,), (1,)), ((), ())), preferred_element_type=F32)


def split(x):
    hi = x.astype(BF16)
    return hi, (x - hi.astype(F32)).astype(BF16)


def kernel(
    n, nv, scale,
    q_h, k_h, v_h, o_h, init_h, upd_h,
    dq_r, dk_r, dv_r, ig_r,
    qv, kv, vv, ov, iv, uv,
    wb, ub, ut, mb, sv, pu, act, tt, rb, vb,
    in_sem, rs_ss, rs_rs, ag_ss, ag_rs, v_ss, v_rs,
):
    hd = iv.shape[1]
    sr = hd // n
    half = n // 2
    rp = min(ROWS_PER_PIECE, sr)
    pieces = [(m, r) for m in range(3) for r in range(0, sr, rp)]

    me = lax.axis_index("tok")
    core = lax.rem(lax.axis_index("head"), 2)
    vid = lax.axis_index("vid")
    flip = lambda i: lax.rem(i * (1 - core) + (n - i) * core, n)
    p = flip(me)
    nxt = flip(lax.rem(p + 1, n))
    prv = flip(lax.rem(p + n - 1, n))

    barrier = pltpu.get_barrier_semaphore()
    for z in (nxt, prv):
        pl.semaphore_signal(barrier, inc=1, device_id={"tok": z}, device_id_type=pl.DeviceIdType.MESH)
    for d in range(1, nv):
        pl.semaphore_signal(
            barrier, inc=1, device_id={"vid": lax.rem(vid + d, nv)}, device_id_type=pl.DeviceIdType.MESH
        )

    loads = {}

    def load(name, src, dst, i):
        loads[name] = pltpu.make_async_copy(src, dst, in_sem.at[i])
        loads[name].start()

    load("init", init_h, iv, 0)
    load("upd0", upd_h.at[0], uv.at[0], 1)
    load("upd1", upd_h.at[1], uv.at[1], 2)
    load("q2", q_h.at[2], qv.at[2], 3)
    load("o2", o_h.at[2], ov.at[2], 4)
    load("k1", k_h.at[1], kv.at[1], 5)
    load("v1", v_h.at[1], vv.at[1], 6)
    load("q1", q_h.at[1], qv.at[1], 7)
    load("o1", o_h.at[1], ov.at[1], 8)
    load("k0", k_h.at[0], kv.at[0], 9)
    load("v0", v_h.at[0], vv.at[0], 10)
    load("q0", q_h.at[0], qv.at[0], 11)
    load("o0", o_h.at[0], ov.at[0], 12)

    def rows(shard, r=0, size=None):
        return pl.ds(pl.multiple_of(lax.rem(shard + 2 * n, n) * sr + r, 8), size or rp)

    def weights():
        for name in ("init", "upd0", "upd1"):
            loads[name].wait()
        for m in range(3):
            w = iv[m].astype(F32)
            for c in range(3):
                hi, lo = split(w)
                wb[c, m, 0] = hi
                wb[c, m, 1] = lo
                if c < 2:
                    up = w + uv[c, m].astype(F32)
                    old = jnp.sqrt(jnp.sum(w * w, axis=0, keepdims=True) + EPS)
                    new = jnp.sqrt(jnp.sum(up * up, axis=0, keepdims=True) + EPS)
                    w = up * (old / new)

    def xw(x, c, m):
        return nn(x, wb[c, m, 0]) + nn(x, wb[c, m, 1])

    def xwt(x, c, m):
        return nt(x, wb[c, m, 0]) + nt(x, wb[c, m, 1])

    def ywt(y, c, m):
        hi, lo = split(y)
        return nt(hi, wb[c, m, 0]) + nt(hi, wb[c, m, 1]) + nt(lo, wb[c, m, 0])

    def yw(y, c, m):
        hi, lo = split(y)
        return nn(hi, wb[c, m, 0]) + nn(hi, wb[c, m, 1]) + nn(lo, wb[c, m, 0])

    def left2(y, x):
        hi, lo = split(y)
        return nn(hi, x) + nn(lo, x)

    def right2(x, y):
        hi, lo = split(y)
        return nn(x, hi) + nn(x, lo)

    def t16(x):
        return x.astype(F32).T.astype(BF16)

    def query_a(c):
        loads[f"q{c}"].wait()
        loads[f"o{c}"].wait()
        g = xw(qv[c], c, 0)
        u = xw(qv[c], c, 1)
        dh = xwt(ov[c], c, 2)
        s = jax.nn.sigmoid(g)
        a = g * s
        act[0] = dh * u * (s * (1.0 + g * (1.0 - s)))
        act[1] = dh * a
        act[2] = a * u

    def query_b(c):
        if c > 0:
            mb[c, 0] = left2(act[0].T, qv[c])
            mb[c, 1] = left2(act[1].T, qv[c])
            mb[c, 2] = right2(t16(ov[c]), act[2])
        else:
            qt = t16(qv[c])
            mb[c, 0] = right2(qt, act[0])
            mb[c, 1] = right2(qt, act[1])
            mb[c, 2] = left2(act[2].T, ov[c])

    def query_c(c):
        dq_r[c] = (ywt(act[0], c, 0) + ywt(act[1], c, 1)).astype(BF16)

    def update_a(c):
        loads[f"k{c}"].wait()
        loads[f"v{c}"].wait()
        g = xw(kv[c], c, 0)
        u = xw(kv[c], c, 1)
        b = xwt(vv[c], c, 2)
        s = jax.nn.sigmoid(g)
        a = g * s * scale
        d1 = (s * (1.0 + g * (1.0 - s))) * scale
        d2 = (s * (1.0 - s) * (2.0 + g * (1.0 - 2.0 * s))) * scale
        act[3] = b * u * d2
        act[4] = b * d1
        act[5] = u * d1
        act[6] = a
        act[7] = b * u * d1
        act[8] = b * a
        act[9] = a * u

    def update_t(c):
        if c > 0:
            tt[...] = t16(vv[c])
        else:
            tt[...] = t16(kv[c])

    def kut(c, m):
        return nt(kv[c], ub[m, 0]) + nt(kv[c], ub[m, 1])

    def update_b(c):
        for m in range(3):
            hi, lo = split(ut[c, m])
            ub[m, 0] = hi
            ub[m, 1] = lo
        d_gate = kut(c, 0)
        d_up = kut(c, 1)
        dh = nn(vv[c], ub[2, 0]) + nn(vv[c], ub[2, 1])
        gb = d_gate * act[3] + d_up * act[4] + dh * act[5]
        u_b = d_gate * act[4] + dh * act[6]
        bb = d_gate * act[5] + d_up * act[6]
        act[0] = gb
        act[1] = u_b
        act[2] = bb
        if c > 0:
            mb[c, 0] += left2(gb.T, kv[c])
            mb[c, 1] += left2(u_b.T, kv[c])
            mb[c, 2] += right2(tt[...], bb)
        else:
            mb[c, 0] += right2(tt[...], gb)
            mb[c, 1] += right2(tt[...], u_b)
            mb[c, 2] += left2(bb.T, vv[c])

    def dot3(y, m, transposed):
        hi, lo = split(y)
        f = nt if transposed else nn
        return f(hi, ub[m, 0]) + f(hi, ub[m, 1]) + f(lo, ub[m, 0])

    def grads_a(c):
        dk_r[c] = (
            dot3(act[7], 0, False) + dot3(act[8], 1, False) + ywt(act[0], c, 0) + ywt(act[1], c, 1)
        ).astype(BF16)

    def grads_b(c):
        dv_r[c] = (dot3(act[9], 2, True) + yw(act[2], c, 2)).astype(BF16)

    def shard_rows():
        at = lax.broadcasted_iota(jnp.int32, (sr, hd), 1) - lax.broadcasted_iota(jnp.int32, (sr, hd), 0)
        pick = jnp.where(at == p * sr, 1.0, 0.0).astype(BF16)
        for m in range(3):
            w = nt(pick, iv[m])
            for c in range(2):
                up = w + nt(pick, uv[c, m])
                old = jnp.sqrt(jnp.sum(w * w, axis=1, keepdims=True) + EPS)
                new = jnp.sqrt(jnp.sum(up * up, axis=1, keepdims=True) + EPS)
                ratio = old / new
                sv[c, 0, m] = up
                sv[c, 1, m] = jnp.broadcast_to(ratio, up.shape)
                sv[c, 2, m] = up * (ratio / (new * new))
                sv[c, 3, m] = w / (old * new)
                w = up * ratio

    def place():
        at = lax.broadcasted_iota(jnp.int32, (sr, hd), 1) - lax.broadcasted_iota(jnp.int32, (sr, hd), 0)
        pick = jnp.where(at == p * sr, 1.0, 0.0)
        for m in range(3):
            mb[0, m] += lax.dot_general(
                pu[m], pick, (((0,), (0,)), ((), ())),
                precision=lax.Precision.HIGHEST, preferred_element_type=F32,
            )

    def copy_to(axis, index, src, dst, ss, rs):
        return pltpu.make_async_remote_copy(
            src_ref=src, dst_ref=dst, send_sem=ss, recv_sem=rs,
            device_id={axis: index}, device_id_type=pl.DeviceIdType.MESH,
        )

    def work(queue):
        if queue:
            queue.pop(0)()

    def reduce_scatter(c, queue, finish):
        sent = []
        for s in range(half):
            for i, (m, r) in enumerate(pieces):
                for d, (to, count) in enumerate(((prv, half), (nxt, n - 1 - half))):
                    if s >= count:
                        continue
                    shard = p - half + s if d == 0 else p + (n - 1 - half) - s
                    own = mb.at[c, m, rows(shard, r)]
                    src = own
                    if s:
                        src = rb.at[c, d, s - 1, m, pl.ds(r, rp)]
                        copy_to("tok", to, src, src, rs_ss.at[d, s - 1, i], rs_rs.at[d, s - 1, i]).wait_recv()
                        src[...] += own[...]
                    cp = copy_to("tok", to, src, rb.at[c, d, s, m, pl.ds(r, rp)], rs_ss.at[d, s, i], rs_rs.at[d, s, i])
                    cp.start()
                    sent.append(cp)
            work(queue)
        for i, (m, r) in enumerate(pieces):
            total = mb[c, m, rows(p, r)]
            for d, count in ((0, half), (1, n - 1 - half)):
                if count:
                    src = rb.at[c, d, count - 1, m, pl.ds(r, rp)]
                    copy_to("tok", nxt, src, src, rs_ss.at[d, count - 1, i], rs_rs.at[d, count - 1, i]).wait_recv()
                    total = total + src[...]
            finish(i, m, r, total)
        for cp in sent:
            cp.wait_send()

    def gather_send(buf, s, i, m, r, d, sent):
        to = nxt if d == 0 else prv
        shard = p - s if d == 0 else p + s
        at = buf.at[m, rows(shard, r)]
        cp = copy_to("tok", to, at, at, ag_ss.at[d, s, i], ag_rs.at[d, s, i])
        cp.start()
        sent.append(cp)

    def gather_rest(buf, queue, sent):
        for s in range(1, half + 1):
            for i, (m, r) in enumerate(pieces):
                for d, count in ((0, half), (1, n - 1 - half)):
                    if s > count:
                        continue
                    shard = p - s if d == 0 else p + s
                    at = buf.at[m, rows(shard, r)]
                    copy_to("tok", nxt, at, at, ag_ss.at[d, s - 1, i], ag_rs.at[d, s - 1, i]).wait_recv()
                    if s < count:
                        gather_send(buf, s, i, m, r, d, sent)
            if s < half:
                work(queue)
        for cp in sent:
            cp.wait_send()

    def norm_back(c, first):
        sent = []

        def finish(i, m, r, total):
            at = pl.ds(r, rp)
            if not first:
                total = total + pu[m, at]
            inner = jnp.sum(total * sv[c, 0, m, at], axis=1, keepdims=True)
            step = total * sv[c, 1, m, at] - inner * sv[c, 2, m, at]
            ut[c, m, rows(p, r)] = step
            gather_send(ut.at[c], 0, i, m, r, 0, sent)
            if n - 1 - half:
                gather_send(ut.at[c], 0, i, m, r, 1, sent)
            pu[m, at] = step + inner * sv[c, 3, m, at]

        return finish, sent

    weights()
    query_a(2)
    query_b(2)
    pl.semaphore_wait(barrier, 2 + nv - 1)

    def zeros():
        dk_r[2] = jnp.zeros(dk_r.shape[1:], BF16)
        dv_r[2] = jnp.zeros(dv_r.shape[1:], BF16)

    finish, sent = norm_back(1, True)
    queue = [
        lambda: (shard_rows(), zeros()), lambda: query_c(2), lambda: update_a(1), lambda: update_t(1),
        lambda: query_a(1), lambda: query_b(1), lambda: query_c(1),
    ]
    reduce_scatter(2, queue, finish)
    gather_rest(ut.at[1], queue, sent)
    while queue:
        work(queue)
    update_b(1)

    finish, sent = norm_back(0, False)
    queue = [
        lambda: grads_a(1), lambda: grads_b(1), lambda: update_a(0), lambda: update_t(0),
        lambda: query_a(0), lambda: query_b(0), lambda: query_c(0),
    ]
    reduce_scatter(1, queue, finish)
    queue.append(place)
    gather_rest(ut.at[0], queue, sent)
    while queue:
        work(queue)
    update_b(0)

    vsent = []
    queue = [lambda: grads_a(0), lambda: grads_b(0)]

    def to_videos(i, m, r, total):
        at = vb.at[vid, m, pl.ds(r, rp)]
        at[...] = total
        for d in range(1, nv):
            cp = copy_to("vid", lax.rem(vid + d, nv), at, at, v_ss.at[d, i], v_rs.at[d, i])
            cp.start()
            vsent.append(cp)

    reduce_scatter(0, queue, to_videos)
    sent = []
    for i, (m, r) in enumerate(pieces):
        for d in range(1, nv):
            at = vb.at[lax.rem(vid + nv - d, nv), m, pl.ds(r, rp)]
            copy_to("vid", vid, at, at, v_ss.at[d, i], v_rs.at[d, i]).wait_recv()
        total = vb[0, m, pl.ds(r, rp)]
        for w in range(1, nv):
            total = total + vb[w, m, pl.ds(r, rp)]
        ig_r[m, rows(p, r)] = total
        gather_send(ig_r, 0, i, m, r, 0, sent)
        if n - 1 - half:
            gather_send(ig_r, 0, i, m, r, 1, sent)
    for cp in vsent:
        cp.wait_send()
    gather_rest(ig_r, queue, sent)


def on_device(n, nv, queries, keys, values, out_grad, fast_init, updates):
    _, groups, tokens, _, hd = queries.shape
    scale = float(tokens * n) ** (-0.5)
    half = n // 2
    sr = hd // n
    pc = 3 * (sr // min(ROWS_PER_PIECE, sr))
    flat = lambda x: x.reshape(groups, tokens, hd)
    anyspec = pl.BlockSpec(memory_space=pl.ANY)
    vspec = pl.BlockSpec(memory_space=pltpu.VMEM)
    dma = pltpu.SemaphoreType.DMA
    tok_shape = jax.ShapeDtypeStruct((groups, tokens, hd), BF16)
    dq, dk, dv, ig = pl.pallas_call(
        functools.partial(kernel, n, nv, scale),
        out_shape=(tok_shape, tok_shape, tok_shape, jax.ShapeDtypeStruct((3, hd, hd), F32)),
        in_specs=[anyspec] * 6,
        out_specs=[vspec] * 4,
        scratch_shapes=[
            pltpu.VMEM((groups, tokens, hd), BF16),
            pltpu.VMEM((groups, tokens, hd), BF16),
            pltpu.VMEM((groups, tokens, hd), BF16),
            pltpu.VMEM((groups, tokens, hd), BF16),
            pltpu.VMEM((3, hd, hd), BF16),
            pltpu.VMEM((2, 3, hd, hd), BF16),
            pltpu.VMEM((3, 3, 2, hd, hd), BF16),
            pltpu.VMEM((3, 2, hd, hd), BF16),
            pltpu.VMEM((2, 3, hd, hd), F32),
            pltpu.VMEM((3, 3, hd, hd), F32),
            pltpu.VMEM((2, 4, 3, sr, hd), F32),
            pltpu.VMEM((3, sr, hd), F32),
            pltpu.VMEM((10, tokens, hd), F32),
            pltpu.VMEM((hd, tokens), BF16),
            pltpu.VMEM((3, 2, half, 3, sr, hd), F32),
            pltpu.VMEM((nv, 3, sr, hd), F32),
            dma((13,)),
            dma((2, half, pc)), dma((2, half, pc)),
            dma((2, half, pc)), dma((2, half, pc)),
            dma((nv, pc)), dma((nv, pc)),
        ],
        compiler_params=pltpu.CompilerParams(
            collective_id=0, has_side_effects=True, vmem_limit_bytes=48 * 1024 * 1024
        ),
    )(
        flat(queries), flat(keys), flat(values), flat(out_grad),
        fast_init.reshape(3, hd, hd), updates.reshape(groups - 1, 3, hd, hd),
    )
    shaped = lambda x: x.reshape(queries.shape)
    return shaped(dq), shaped(dk), shaped(dv), ig.reshape(fast_init.shape)


def solution(mesh):
    return jax.shard_map(
        functools.partial(on_device, mesh.shape["tok"], mesh.shape["vid"]),
        mesh=mesh,
        in_specs=(
            P("vid", None, "tok", "head", None),
            P("vid", None, "tok", "head", None),
            P("vid", None, "tok", "head", None),
            P("vid", None, "tok", "head", None),
            P("head", None, None, None),
            P("vid", None, "head", None, None, None),
        ),
        out_specs=(
            P("vid", None, "tok", "head", None),
            P("vid", None, "tok", "head", None),
            P("vid", None, "tok", "head", None),
            P("head", None, None, None),
        ),
        check_vma=False,
    )
```

```python
import functools

import jax
import jax.numpy as jnp
from jax import lax
from jax.experimental import pallas as pl
from jax.experimental.pallas import tpu as pltpu
from jax.sharding import PartitionSpec as P

EPS = 1e-06
F32 = jnp.float32
BF16 = jnp.bfloat16
TREE = {1: 0, 3: 0, 2: 1, 4: 3, 6: 3, 5: 4, 7: 6, 8: 6}
FIXED, HOP = 2.2, 0.9
STAGGER = 1.0


def tree(n):
    half = n // 2
    if half == 8:
        up = dict(TREE)
    else:
        up = {d: d - 1 for d in range(1, half + 1)}
    parent = dict(up)
    for d, to in up.items():
        if d < n - half:
            parent[-d] = -to
    return parent


def depth(parent):
    t = {0: 0.0}
    for d in sorted(parent, key=lambda d: (abs(d), d)):
        chain = [d]
        while chain[-1] not in t:
            chain.append(parent[chain[-1]])
        for a, b in zip(chain[-2::-1], chain[:0:-1]):
            t[a] = t[b] + FIXED + HOP * abs(a - b)
    return t


def nn(a, b):
    return lax.dot_general(a, b, (((1,), (0,)), ((), ())), preferred_element_type=F32)


def nt(a, b):
    return lax.dot_general(a, b, (((1,), (1,)), ((), ())), preferred_element_type=F32)


def split(x):
    hi = x.astype(BF16)
    return hi, (x - hi.astype(F32)).astype(BF16)


def kernel(
    n, nv, scale, parent,
    q_h, k_h, v_h, o_h, init_h, upd_h,
    dq_r, dk_r, dv_r, ig_r,
    qv, kv, vv, ov, iv, uv,
    wb, ub, ut, mb, sv, pu, act, tt, rb, vb,
    in_sem, rs_ss, rs_rs, ag_ss, ag_rs, v_ss, v_rs,
):
    hd = iv.shape[1]
    sr = hd // n
    index = {d: i for i, d in enumerate(parent)}
    kids = {d: sorted((e for e in parent if parent[e] == d), key=lambda e: -abs(e)) for d in [0] + list(parent)}
    when = depth(parent)
    span = max(when.values())

    me = lax.axis_index("tok")
    core = lax.rem(lax.axis_index("head"), 2)
    vid = lax.axis_index("vid")
    flip = lambda i: lax.rem(i * (1 - core) + (n - i) * core, n)
    p = flip(me)
    jumps = sorted({(d - parent[d]) % n for d in parent} | {(parent[d] - d) % n for d in parent})
    device = {j: flip(lax.rem(p + j, n)) for j in jumps}

    barrier = pltpu.get_barrier_semaphore()
    for j in jumps:
        pl.semaphore_signal(barrier, inc=1, device_id={"tok": device[j]}, device_id_type=pl.DeviceIdType.MESH)
    for d in range(1, nv):
        pl.semaphore_signal(
            barrier, inc=1, device_id={"vid": lax.rem(vid + d, nv)}, device_id_type=pl.DeviceIdType.MESH
        )

    loads = {}

    def load(name, src, dst, i):
        loads[name] = pltpu.make_async_copy(src, dst, in_sem.at[i])
        loads[name].start()

    load("init", init_h, iv, 0)
    load("upd0", upd_h.at[0], uv.at[0], 1)
    load("upd1", upd_h.at[1], uv.at[1], 2)
    load("q2", q_h.at[2], qv.at[2], 3)
    load("o2", o_h.at[2], ov.at[2], 4)
    load("k1", k_h.at[1], kv.at[1], 5)
    load("v1", v_h.at[1], vv.at[1], 6)
    load("q1", q_h.at[1], qv.at[1], 7)
    load("o1", o_h.at[1], ov.at[1], 8)
    load("k0", k_h.at[0], kv.at[0], 9)
    load("v0", v_h.at[0], vv.at[0], 10)
    load("q0", q_h.at[0], qv.at[0], 11)
    load("o0", o_h.at[0], ov.at[0], 12)

    def rows(shard):
        return pl.ds(pl.multiple_of(lax.rem(shard + 2 * n, n) * sr, 8), sr)

    def weights(m):
        w = iv[m].astype(F32)
        for c in range(3):
            hi, lo = split(w)
            wb[c, m, 0] = hi
            wb[c, m, 1] = lo
            if c < 2:
                up = w + uv[c, m].astype(F32)
                old = jnp.sqrt(jnp.sum(w * w, axis=0, keepdims=True) + EPS)
                new = jnp.sqrt(jnp.sum(up * up, axis=0, keepdims=True) + EPS)
                w = up * (old / new)

    def xw(x, c, m):
        return nn(x, wb[c, m, 0]) + nn(x, wb[c, m, 1])

    def xwt(x, c, m):
        return nt(x, wb[c, m, 0]) + nt(x, wb[c, m, 1])

    def ywt(y, c, m):
        hi, lo = split(y)
        return nt(hi, wb[c, m, 0]) + nt(hi, wb[c, m, 1]) + nt(lo, wb[c, m, 0])

    def yw(y, c, m):
        hi, lo = split(y)
        return nn(hi, wb[c, m, 0]) + nn(hi, wb[c, m, 1]) + nn(lo, wb[c, m, 0])

    def left2(y, x):
        hi, lo = split(y)
        return nn(hi, x) + nn(lo, x)

    def right2(x, y):
        hi, lo = split(y)
        return nn(x, hi) + nn(x, lo)

    def t16(x):
        return x.astype(F32).T.astype(BF16)

    def query_a(c):
        loads[f"q{c}"].wait()
        g = xw(qv[c], c, 0)
        u = xw(qv[c], c, 1)
        s = jax.nn.sigmoid(g)
        a = g * s
        act[0] = u * (s * (1.0 + g * (1.0 - s)))
        act[1] = a
        act[2] = a * u

    def query_d(c):
        dh = xwt(ov[c], c, 2)
        act[0] = dh * act[0]
        act[1] = dh * act[1]

    def query_sum(c, m):
        if m == 2:
            loads[f"o{c}"].wait()
            mb[c, 2] = right2(t16(ov[c]), act[2]) if c else left2(act[2].T, ov[c])
        else:
            mb[c, m] = left2(act[m].T, qv[c]) if c else right2(t16(qv[c]), act[m])

    def query_c(c):
        dq_r[c] = (ywt(act[0], c, 0) + ywt(act[1], c, 1)).astype(BF16)

    def update_a(c):
        loads[f"k{c}"].wait()
        loads[f"v{c}"].wait()
        g = xw(kv[c], c, 0)
        u = xw(kv[c], c, 1)
        b = xwt(vv[c], c, 2)
        s = jax.nn.sigmoid(g)
        a = g * s * scale
        d1 = (s * (1.0 + g * (1.0 - s))) * scale
        d2 = (s * (1.0 - s) * (2.0 + g * (1.0 - 2.0 * s))) * scale
        act[3] = b * u * d2
        act[4] = b * d1
        act[5] = u * d1
        act[6] = a
        act[7] = b * u * d1
        act[8] = b * a
        act[9] = a * u

    def update_t(c):
        if c > 0:
            tt[...] = t16(vv[c])
        else:
            tt[...] = t16(kv[c])

    def kut(c, m):
        return nt(kv[c], ub[m, 0]) + nt(kv[c], ub[m, 1])

    def halves(c, m):
        hi, lo = split(ut[c, m])
        ub[m, 0] = hi
        ub[m, 1] = lo

    def after_gate(c):
        halves(c, 0)
        act[10] = kut(c, 0)

    def after_up(c):
        halves(c, 1)
        act[11] = kut(c, 1)

    def after_down(c):
        halves(c, 2)
        act[12] = nn(vv[c], ub[2, 0]) + nn(vv[c], ub[2, 1])

    def sum_gate(c):
        y = act[10] * act[3] + act[11] * act[4] + act[12] * act[5]
        act[0] = y
        mb[c, 0] += left2(y.T, kv[c]) if c else right2(tt[...], y)

    def sum_up(c):
        y = act[10] * act[4] + act[12] * act[6]
        act[1] = y
        mb[c, 1] += left2(y.T, kv[c]) if c else right2(tt[...], y)

    def sum_down(c):
        y = act[10] * act[5] + act[11] * act[6]
        act[2] = y
        mb[c, 2] += right2(tt[...], y) if c else left2(y.T, vv[c])

    def dot3(y, m, transposed):
        hi, lo = split(y)
        f = nt if transposed else nn
        return f(hi, ub[m, 0]) + f(hi, ub[m, 1]) + f(lo, ub[m, 0])

    def grads_a(c):
        dk_r[c] = (
            dot3(act[7], 0, False) + dot3(act[8], 1, False) + ywt(act[0], c, 0) + ywt(act[1], c, 1)
        ).astype(BF16)

    def grads_b(c):
        dv_r[c] = (dot3(act[9], 2, True) + yw(act[2], c, 2)).astype(BF16)

    def shard_rows():
        at = lax.broadcasted_iota(jnp.int32, (sr, hd), 1) - lax.broadcasted_iota(jnp.int32, (sr, hd), 0)
        pick = jnp.where(at == p * sr, 1.0, 0.0).astype(BF16)
        for m in range(3):
            w = nt(pick, iv[m])
            for c in range(2):
                up = w + nt(pick, uv[c, m])
                old = jnp.sqrt(jnp.sum(w * w, axis=1, keepdims=True) + EPS)
                new = jnp.sqrt(jnp.sum(up * up, axis=1, keepdims=True) + EPS)
                ratio = old / new
                sv[c, 0, m] = up
                sv[c, 1, m] = jnp.broadcast_to(ratio, up.shape)
                sv[c, 2, m] = up * (ratio / (new * new))
                sv[c, 3, m] = w / (old * new)
                w = up * ratio

    def place():
        at = lax.broadcasted_iota(jnp.int32, (sr, hd), 1) - lax.broadcasted_iota(jnp.int32, (sr, hd), 0)
        pick = jnp.where(at == p * sr, 1.0, 0.0)
        for m in range(3):
            mb[0, m] += lax.dot_general(
                pu[m], pick, (((0,), (0,)), ((), ())),
                precision=lax.Precision.HIGHEST, preferred_element_type=F32,
            )

    def copy_to(axis, index, src, dst, ss, rs):
        return pltpu.make_async_remote_copy(
            src_ref=src, dst_ref=dst, send_sem=ss, recv_sem=rs,
            device_id={axis: index}, device_id_type=pl.DeviceIdType.MESH,
        )

    sent = []

    def arrived(at, sem):
        copy_to("tok", device[jumps[0]], at, at, sem, sem).wait_recv()

    def collect(c, m, d):
        own = mb.at[c, m, rows(p - d)]
        if not kids[d]:
            return own
        total = None
        for e in kids[d]:
            at = rb.at[c, index[e], m]
            arrived(at, rs_rs.at[c, index[e], m])
            total = (own[...] if total is None else total) + at[...]
        if d == 0:
            return total
        at = rb.at[c, index[kids[d][0]], m]
        at[...] = total
        return at

    def reduce_send(c, m, d):
        i = index[d]
        cp = copy_to(
            "tok", device[(parent[d] - d) % n], collect(c, m, d), rb.at[c, i, m], rs_ss.at[c, i, m], rs_rs.at[c, i, m]
        )
        cp.start()
        sent.append(cp)

    def gather_send(c, buf, m, d):
        at = buf.at[m, rows(p - d)]
        for e in kids[d]:
            cp = copy_to(
                "tok", device[(e - d) % n], at, at, ag_ss.at[c, index[e], m], ag_rs.at[c, index[e], m]
            )
            cp.start()
            sent.append(cp)

    def gather_step(c, buf, m, d):
        arrived(buf.at[m, rows(p - d)], ag_rs.at[c, index[d], m])
        gather_send(c, buf, m, d)

    def norm_back(c, m, first):
        total = collect(c + 1, m, 0)
        if not first:
            total = total + pu[m]
        inner = jnp.sum(total * sv[c, 0, m], axis=1, keepdims=True)
        step = total * sv[c, 1, m] - inner * sv[c, 2, m]
        ut[c, m, rows(p)] = step
        gather_send(c + 1, ut.at[c], m, 0)
        pu[m] = step + inner * sv[c, 3, m]

    def to_videos(m):
        at = vb.at[vid, m]
        at[...] = collect(0, m, 0)
        for d in range(1, nv):
            cp = copy_to("vid", lax.rem(vid + d, nv), at, at, v_ss.at[d, m], v_rs.at[d, m])
            cp.start()
            sent.append(cp)

    def from_videos(m):
        for d in range(1, nv):
            arrived(vb.at[lax.rem(vid + nv - d, nv), m], v_rs.at[d, m])
        total = vb[0, m]
        for w in range(1, nv):
            total = total + vb[w, m]
        ig_r[m, rows(p)] = total
        gather_send(0, ig_r, m, 0)

    events = []
    queue = []

    def at(t, f, *args):
        events.append((t, len(events), functools.partial(f, *args)))

    def later(*fs):
        queue.extend(fs)

    def flush():
        while queue:
            queue.pop(0)()

    def exchange(c, starts, finish, extra, buf):
        ends = {}
        for m, t in starts.items():
            for d in parent:
                at(t + span - when[d], reduce_send, c, m, d)
            t += span + 0.2
            at(t, finish, m)
            if extra:
                t += extra
                at(t, from_videos, m)
            for d in parent:
                at(t + 0.2 + when[d], gather_step, c, buf, m, d)
            ends[m] = t + 0.2 + span
        return ends

    done = set()

    def once(f, *args):
        if (f, args) not in done:
            done.add((f, args))
            f(*args)

    def zeros():
        dk_r[2] = jnp.zeros(dk_r.shape[1:], BF16)
        dv_r[2] = jnp.zeros(dv_r.shape[1:], BF16)

    for name in ("init", "upd0", "upd1"):
        loads[name].wait()
    weights(0)
    weights(1)
    query_a(2)
    query_sum(2, 2)
    pl.semaphore_wait(barrier, len(jumps) + nv - 1)

    def first_rest():
        weights(2)
        query_d(2)
        query_sum(2, 0)

    at(0.01, first_rest)
    at(STAGGER - 0.01, query_sum, 2, 1)
    later(
        functools.partial(once, shard_rows), lambda: query_c(2), lambda: update_a(1), lambda: update_t(1),
        lambda: query_a(1), lambda: query_sum(1, 2), lambda: query_d(1), lambda: query_sum(1, 0),
        lambda: query_sum(1, 1), lambda: query_c(1), zeros,
    )
    ends = exchange(
        2, {2: 0.0, 0: STAGGER, 1: 2 * STAGGER},
        lambda m: (once(shard_rows), norm_back(1, m, True)), 0, ut.at[1],
    )
    at(ends[2] + 0.01, lambda: (flush(), after_down(1)))
    at(ends[0] + 0.01, lambda: (after_gate(1), sum_up(1)))
    at(ends[1] + 0.01, lambda: (after_up(1), sum_down(1)))
    t1 = {1: ends[0] + 0.5, 2: ends[1] + 0.5, 0: ends[1] + 0.5 + STAGGER}
    at(t1[2] + 0.01, lambda: (sum_gate(1), later(
        lambda: grads_a(1), lambda: grads_b(1), lambda: update_a(0), lambda: update_t(0),
        lambda: query_a(0), lambda: query_sum(0, 2), lambda: query_d(0), lambda: query_sum(0, 0),
        lambda: query_sum(0, 1), lambda: query_c(0),
    )))
    ends = exchange(1, t1, lambda m: norm_back(0, m, False), 0, ut.at[0])
    at(max(t1.values()) + span + 0.3, later, place)
    at(ends[1] + 0.01, lambda: (flush(), after_up(0)))
    at(ends[2] + 0.01, after_down, 0)
    at(ends[0] + 0.01, lambda: (after_gate(0), sum_up(0)))
    t0 = {1: ends[0] + 0.5, 2: ends[0] + 0.5 + STAGGER, 0: ends[0] + 0.5 + 2 * STAGGER}
    at(t0[1] + 0.01, sum_down, 0)
    at(t0[2] + 0.01, lambda: (sum_gate(0), later(lambda: grads_a(0), lambda: grads_b(0))))
    exchange(0, t0, to_videos, FIXED + 2 * HOP, ig_r)

    events.sort(key=lambda e: e[:2])
    for (t, _, f), after in zip(events, events[1:] + [(events[-1][0] + 9.0,)]):
        f()
        gap = after[0] - t
        while queue and gap > 0.45:
            queue.pop(0)()
            gap -= 0.7
    flush()
    for cp in sent:
        cp.wait_send()


def on_device(n, nv, queries, keys, values, out_grad, fast_init, updates):
    _, groups, tokens, _, hd = queries.shape
    scale = float(tokens * n) ** (-0.5)
    sr = hd // n
    parent = tree(n)
    edges = len(parent)
    flat = lambda x: x.reshape(groups, tokens, hd)
    hbm = pl.BlockSpec(memory_space=pltpu.HBM)
    vspec = pl.BlockSpec(memory_space=pltpu.VMEM)
    dma = pltpu.SemaphoreType.DMA
    tok_shape = jax.ShapeDtypeStruct((groups, tokens, hd), BF16)
    dq, dk, dv, ig = pl.pallas_call(
        functools.partial(kernel, n, nv, scale, parent),
        out_shape=(tok_shape, tok_shape, tok_shape, jax.ShapeDtypeStruct((3, hd, hd), F32)),
        in_specs=[hbm] * 6,
        out_specs=[vspec] * 4,
        scratch_shapes=[
            pltpu.VMEM((groups, tokens, hd), BF16),
            pltpu.VMEM((groups, tokens, hd), BF16),
            pltpu.VMEM((groups, tokens, hd), BF16),
            pltpu.VMEM((groups, tokens, hd), BF16),
            pltpu.VMEM((3, hd, hd), BF16),
            pltpu.VMEM((2, 3, hd, hd), BF16),
            pltpu.VMEM((3, 3, 2, hd, hd), BF16),
            pltpu.VMEM((3, 2, hd, hd), BF16),
            pltpu.VMEM((2, 3, hd, hd), F32),
            pltpu.VMEM((3, 3, hd, hd), F32),
            pltpu.VMEM((2, 4, 3, sr, hd), F32),
            pltpu.VMEM((3, sr, hd), F32),
            pltpu.VMEM((13, tokens, hd), F32),
            pltpu.VMEM((hd, tokens), BF16),
            pltpu.VMEM((3, edges, 3, sr, hd), F32),
            pltpu.VMEM((nv, 3, sr, hd), F32),
            dma((13,)),
            dma((3, edges, 3)), dma((3, edges, 3)),
            dma((3, edges, 3)), dma((3, edges, 3)),
            dma((nv, 3)), dma((nv, 3)),
        ],
        compiler_params=pltpu.CompilerParams(
            collective_id=0, has_side_effects=True, vmem_limit_bytes=48 * 1024 * 1024
        ),
    )(
        flat(queries), flat(keys), flat(values), flat(out_grad),
        fast_init.reshape(3, hd, hd), updates.reshape(groups - 1, 3, hd, hd),
    )
    shaped = lambda x: x.reshape(queries.shape)
    return shaped(dq), shaped(dk), shaped(dv), ig.reshape(fast_init.shape)


def solution(mesh):
    return jax.shard_map(
        functools.partial(on_device, mesh.shape["tok"], mesh.shape["vid"]),
        mesh=mesh,
        in_specs=(
            P("vid", None, "tok", "head", None),
            P("vid", None, "tok", "head", None),
            P("vid", None, "tok", "head", None),
            P("vid", None, "tok", "head", None),
            P("head", None, None, None),
            P("vid", None, "head", None, None, None),
        ),
        out_specs=(
            P("vid", None, "tok", "head", None),
            P("vid", None, "tok", "head", None),
            P("vid", None, "tok", "head", None),
            P("head", None, None, None),
        ),
        check_vma=False,
    )
```

```python
import functools

import jax
import jax.numpy as jnp
from jax import lax
from jax.experimental import pallas as pl
from jax.experimental.pallas import tpu as pltpu
from jax.sharding import PartitionSpec as P

EPS = 1e-06
F32 = jnp.float32
BF16 = jnp.bfloat16
TREE = {1: 0, 3: 0, 2: 1, 4: 3, 6: 3, 5: 4, 7: 6, 8: 6}
FIXED, HOP = 4.5, 0.4
STAGGER = 1.5


def tree(n):
    half = n // 2
    if half == 8:
        up = dict(TREE)
    else:
        up = {d: d - 1 for d in range(1, half + 1)}
    parent = dict(up)
    for d, to in up.items():
        if d < n - half:
            parent[-d] = -to
    return parent


def depth(parent):
    t = {0: 0.0}
    for d in sorted(parent, key=lambda d: (abs(d), d)):
        chain = [d]
        while chain[-1] not in t:
            chain.append(parent[chain[-1]])
        for a, b in zip(chain[-2::-1], chain[:0:-1]):
            t[a] = t[b] + FIXED + HOP * abs(a - b)
    return t


def nn(a, b):
    return lax.dot_general(a, b, (((1,), (0,)), ((), ())), preferred_element_type=F32)


def nt(a, b):
    return lax.dot_general(a, b, (((1,), (1,)), ((), ())), preferred_element_type=F32)


def split(x):
    hi = x.astype(BF16)
    return hi, (x - hi.astype(F32)).astype(BF16)


def kernel(
    n, nv, scale, parent,
    q_h, k_h, v_h, o_h, init_h, upd_h,
    dq_r, dk_r, dv_r, ig_r,
    qv, kv, vv, ov, iv, uv,
    wb, ub, ut, mb, sv, pu, act, tt, rb, vb,
    in_sem, rs_ss, rs_rs, ag_ss, ag_rs, v_ss, v_rs,
):
    hd = iv.shape[1]
    sr = hd // n
    index = {d: i for i, d in enumerate(parent)}
    kids = {d: sorted((e for e in parent if parent[e] == d), key=lambda e: -abs(e)) for d in [0] + list(parent)}
    when = depth(parent)
    span = max(when.values())

    me = lax.axis_index("tok")
    core = lax.rem(lax.axis_index("head"), 2)
    vid = lax.axis_index("vid")
    flip = lambda i: lax.rem(i * (1 - core) + (n - i) * core, n)
    p = flip(me)
    jumps = sorted({(d - parent[d]) % n for d in parent} | {(parent[d] - d) % n for d in parent})
    device = {j: flip(lax.rem(p + j, n)) for j in jumps}

    barrier = pltpu.get_barrier_semaphore()
    for j in jumps:
        pl.semaphore_signal(barrier, inc=1, device_id={"tok": device[j]}, device_id_type=pl.DeviceIdType.MESH)
    for d in range(1, nv):
        pl.semaphore_signal(
            barrier, inc=1, device_id={"vid": lax.rem(vid + d, nv)}, device_id_type=pl.DeviceIdType.MESH
        )

    loads = {}

    def load(name, src, dst, i):
        loads[name] = pltpu.make_async_copy(src, dst, in_sem.at[i])
        loads[name].start()

    load("init", init_h, iv, 0)
    load("upd0", upd_h.at[0], uv.at[0], 1)
    load("upd1", upd_h.at[1], uv.at[1], 2)
    load("q2", q_h.at[2], qv.at[2], 3)
    load("o2", o_h.at[2], ov.at[2], 4)
    load("k1", k_h.at[1], kv.at[1], 5)
    load("v1", v_h.at[1], vv.at[1], 6)
    load("q1", q_h.at[1], qv.at[1], 7)
    load("o1", o_h.at[1], ov.at[1], 8)
    load("k0", k_h.at[0], kv.at[0], 9)
    load("v0", v_h.at[0], vv.at[0], 10)
    load("q0", q_h.at[0], qv.at[0], 11)
    load("o0", o_h.at[0], ov.at[0], 12)

    def rows(shard):
        return pl.ds(pl.multiple_of(lax.rem(shard + 2 * n, n) * sr, 8), sr)

    def weights(m):
        w = iv[m].astype(F32)
        for c in range(3):
            hi, lo = split(w)
            wb[c, m, 0] = hi
            wb[c, m, 1] = lo
            if c < 2:
                up = w + uv[c, m].astype(F32)
                old = jnp.sqrt(jnp.sum(w * w, axis=0, keepdims=True) + EPS)
                new = jnp.sqrt(jnp.sum(up * up, axis=0, keepdims=True) + EPS)
                w = up * (old / new)

    def xw(x, c, m):
        return nn(x, wb[c, m, 0]) + nn(x, wb[c, m, 1])

    def xwt(x, c, m):
        return nt(x, wb[c, m, 0]) + nt(x, wb[c, m, 1])

    def ywt(y, c, m):
        hi, lo = split(y)
        return nt(hi, wb[c, m, 0]) + nt(hi, wb[c, m, 1]) + nt(lo, wb[c, m, 0])

    def yw(y, c, m):
        hi, lo = split(y)
        return nn(hi, wb[c, m, 0]) + nn(hi, wb[c, m, 1]) + nn(lo, wb[c, m, 0])

    def left2(y, x):
        hi, lo = split(y)
        return nn(hi, x) + nn(lo, x)

    def right2(x, y):
        hi, lo = split(y)
        return nn(x, hi) + nn(x, lo)

    def t16(x):
        return x.astype(F32).T.astype(BF16)

    def query_a(c):
        loads[f"q{c}"].wait()
        g = xw(qv[c], c, 0)
        u = xw(qv[c], c, 1)
        s = jax.nn.sigmoid(g)
        a = g * s
        act[0] = u * (s * (1.0 + g * (1.0 - s)))
        act[1] = a
        act[2] = a * u

    def query_d(c):
        dh = xwt(ov[c], c, 2)
        act[0] = dh * act[0]
        act[1] = dh * act[1]

    def query_sum(c, m):
        if m == 2:
            loads[f"o{c}"].wait()
            mb[c, 2] = right2(t16(ov[c]), act[2]) if c else left2(act[2].T, ov[c])
        else:
            mb[c, m] = left2(act[m].T, qv[c]) if c else right2(t16(qv[c]), act[m])

    def query_c(c):
        dq_r[c] = (ywt(act[0], c, 0) + ywt(act[1], c, 1)).astype(BF16)

    def update_a(c):
        loads[f"k{c}"].wait()
        loads[f"v{c}"].wait()
        g = xw(kv[c], c, 0)
        u = xw(kv[c], c, 1)
        b = xwt(vv[c], c, 2)
        s = jax.nn.sigmoid(g)
        a = g * s * scale
        d1 = (s * (1.0 + g * (1.0 - s))) * scale
        d2 = (s * (1.0 - s) * (2.0 + g * (1.0 - 2.0 * s))) * scale
        act[3] = b * u * d2
        act[4] = b * d1
        act[5] = u * d1
        act[6] = a
        act[7] = b * u * d1
        act[8] = b * a
        act[9] = a * u

    def update_t(c):
        if c > 0:
            tt[...] = t16(vv[c])
        else:
            tt[...] = t16(kv[c])

    def kut(c, m):
        return nt(kv[c], ub[m, 0]) + nt(kv[c], ub[m, 1])

    def halves(c, m):
        hi, lo = split(ut[c, m])
        ub[m, 0] = hi
        ub[m, 1] = lo

    def after_gate(c):
        halves(c, 0)
        act[10] = kut(c, 0)

    def after_up(c):
        halves(c, 1)
        act[11] = kut(c, 1)

    def after_down(c):
        halves(c, 2)
        act[12] = nn(vv[c], ub[2, 0]) + nn(vv[c], ub[2, 1])

    def sum_gate(c):
        y = act[10] * act[3] + act[11] * act[4] + act[12] * act[5]
        act[0] = y
        mb[c, 0] += left2(y.T, kv[c]) if c else right2(tt[...], y)

    def sum_up(c):
        y = act[10] * act[4] + act[12] * act[6]
        act[1] = y
        mb[c, 1] += left2(y.T, kv[c]) if c else right2(tt[...], y)

    def sum_down(c):
        y = act[10] * act[5] + act[11] * act[6]
        act[2] = y
        mb[c, 2] += right2(tt[...], y) if c else left2(y.T, vv[c])

    def dot3(y, m, transposed):
        hi, lo = split(y)
        f = nt if transposed else nn
        return f(hi, ub[m, 0]) + f(hi, ub[m, 1]) + f(lo, ub[m, 0])

    def grads_a(c):
        dk_r[c] = (
            dot3(act[7], 0, False) + dot3(act[8], 1, False) + ywt(act[0], c, 0) + ywt(act[1], c, 1)
        ).astype(BF16)

    def grads_b(c):
        dv_r[c] = (dot3(act[9], 2, True) + yw(act[2], c, 2)).astype(BF16)

    def shard_rows():
        at = lax.broadcasted_iota(jnp.int32, (sr, hd), 1) - lax.broadcasted_iota(jnp.int32, (sr, hd), 0)
        pick = jnp.where(at == p * sr, 1.0, 0.0).astype(BF16)
        for m in range(3):
            w = nt(pick, iv[m])
            for c in range(2):
                up = w + nt(pick, uv[c, m])
                old = jnp.sqrt(jnp.sum(w * w, axis=1, keepdims=True) + EPS)
                new = jnp.sqrt(jnp.sum(up * up, axis=1, keepdims=True) + EPS)
                ratio = old / new
                sv[c, 0, m] = up
                sv[c, 1, m] = jnp.broadcast_to(ratio, up.shape)
                sv[c, 2, m] = up * (ratio / (new * new))
                sv[c, 3, m] = w / (old * new)
                w = up * ratio

    def place():
        at = lax.broadcasted_iota(jnp.int32, (sr, hd), 1) - lax.broadcasted_iota(jnp.int32, (sr, hd), 0)
        pick = jnp.where(at == p * sr, 1.0, 0.0)
        for m in range(3):
            mb[0, m] += lax.dot_general(
                pu[m], pick, (((0,), (0,)), ((), ())),
                precision=lax.Precision.HIGHEST, preferred_element_type=F32,
            )

    def copy_to(axis, index, src, dst, ss, rs):
        return pltpu.make_async_remote_copy(
            src_ref=src, dst_ref=dst, send_sem=ss, recv_sem=rs,
            device_id={axis: index}, device_id_type=pl.DeviceIdType.MESH,
        )

    sent = []

    def arrived(at, sem):
        copy_to("tok", device[jumps[0]], at, at, sem, sem).wait_recv()

    def collect(c, m, d):
        own = mb.at[c, m, rows(p - d)]
        if not kids[d]:
            return own
        total = None
        for e in kids[d]:
            at = rb.at[c, index[e], m]
            arrived(at, rs_rs.at[c, index[e], m])
            total = (own[...] if total is None else total) + at[...]
        if d == 0:
            return total
        at = rb.at[c, index[kids[d][0]], m]
        at[...] = total
        return at

    def reduce_send(c, m, d):
        i = index[d]
        cp = copy_to(
            "tok", device[(parent[d] - d) % n], collect(c, m, d), rb.at[c, i, m], rs_ss.at[c, i, m], rs_rs.at[c, i, m]
        )
        cp.start()
        sent.append(cp)

    def gather_send(c, buf, m, d):
        at = buf.at[m, rows(p - d)]
        for e in kids[d]:
            cp = copy_to(
                "tok", device[(e - d) % n], at, at, ag_ss.at[c, index[e], m], ag_rs.at[c, index[e], m]
            )
            cp.start()
            sent.append(cp)

    def gather_step(c, buf, m, d):
        arrived(buf.at[m, rows(p - d)], ag_rs.at[c, index[d], m])
        gather_send(c, buf, m, d)

    def norm_back(c, m, first):
        total = collect(c + 1, m, 0)
        if not first:
            total = total + pu[m]
        inner = jnp.sum(total * sv[c, 0, m], axis=1, keepdims=True)
        step = total * sv[c, 1, m] - inner * sv[c, 2, m]
        ut[c, m, rows(p)] = step
        gather_send(c + 1, ut.at[c], m, 0)
        pu[m] = step + inner * sv[c, 3, m]

    def to_videos(m):
        at = vb.at[vid, m]
        at[...] = collect(0, m, 0)
        for d in range(1, nv):
            cp = copy_to("vid", lax.rem(vid + d, nv), at, at, v_ss.at[d, m], v_rs.at[d, m])
            cp.start()
            sent.append(cp)

    def from_videos(m):
        for d in range(1, nv):
            arrived(vb.at[lax.rem(vid + nv - d, nv), m], v_rs.at[d, m])
        total = vb[0, m]
        for w in range(1, nv):
            total = total + vb[w, m]
        ig_r[m, rows(p)] = total
        gather_send(0, ig_r, m, 0)

    events = []
    queue = []

    def at(t, f, *args):
        events.append((t, len(events), functools.partial(f, *args)))

    def later(*fs):
        queue.extend(fs)

    def flush():
        while queue:
            queue.pop(0)()

    def exchange(c, starts, finish, extra, buf):
        ends = {}
        for m, t in starts.items():
            for d in parent:
                at(t + span - when[d], reduce_send, c, m, d)
            t += span + 0.2
            at(t, finish, m)
            if extra:
                t += extra
                at(t, from_videos, m)
            for d in parent:
                at(t + 0.2 + when[d], gather_step, c, buf, m, d)
            ends[m] = t + 0.2 + span
        return ends

    done = set()

    def once(f, *args):
        if (f, args) not in done:
            done.add((f, args))
            f(*args)

    def zeros():
        dk_r[2] = jnp.zeros(dk_r.shape[1:], BF16)
        dv_r[2] = jnp.zeros(dv_r.shape[1:], BF16)

    for name in ("init", "upd0", "upd1"):
        loads[name].wait()
    weights(0)
    weights(1)
    query_a(2)
    query_sum(2, 2)
    pl.semaphore_wait(barrier, len(jumps) + nv - 1)

    def first_rest():
        weights(2)
        query_d(2)
        query_sum(2, 0)

    at(0.01, first_rest)
    at(STAGGER - 0.01, query_sum, 2, 1)
    later(
        functools.partial(once, shard_rows), lambda: query_c(2), lambda: update_a(1), lambda: update_t(1),
        lambda: query_a(1), lambda: query_sum(1, 2), lambda: query_d(1), lambda: query_sum(1, 0),
        lambda: query_sum(1, 1), lambda: query_c(1), zeros,
    )
    ends = exchange(
        2, {2: 0.0, 0: STAGGER, 1: 2 * STAGGER},
        lambda m: (once(shard_rows), norm_back(1, m, True)), 0, ut.at[1],
    )
    at(ends[2] + 0.01, lambda: (flush(), after_down(1)))
    at(ends[0] + 0.01, lambda: (after_gate(1), sum_up(1)))
    at(ends[1] + 0.01, lambda: (after_up(1), sum_down(1)))
    t1 = {1: ends[0] + 0.5, 2: ends[1] + 0.5, 0: ends[1] + 0.5 + STAGGER}
    at(t1[2] + 0.01, lambda: (sum_gate(1), later(
        lambda: grads_a(1), lambda: grads_b(1), lambda: update_a(0), lambda: update_t(0),
        lambda: query_a(0), lambda: query_sum(0, 2), lambda: query_d(0), lambda: query_sum(0, 0),
        lambda: query_sum(0, 1), lambda: query_c(0),
    )))
    ends = exchange(1, t1, lambda m: norm_back(0, m, False), 0, ut.at[0])
    at(max(t1.values()) + span + 0.3, later, place)
    at(ends[1] + 0.01, lambda: (flush(), after_up(0)))
    at(ends[2] + 0.01, after_down, 0)
    at(ends[0] + 0.01, lambda: (after_gate(0), sum_up(0)))
    t0 = {1: ends[0] + 0.5, 2: ends[0] + 0.5 + STAGGER, 0: ends[0] + 0.5 + 2 * STAGGER}
    at(t0[1] + 0.01, sum_down, 0)
    at(t0[2] + 0.01, lambda: (sum_gate(0), later(lambda: grads_a(0), lambda: grads_b(0))))
    exchange(0, t0, to_videos, FIXED + 2 * HOP, ig_r)

    events.sort(key=lambda e: e[:2])
    for (t, _, f), after in zip(events, events[1:] + [(events[-1][0] + 9.0,)]):
        f()
        gap = after[0] - t
        while queue and gap > 0.45:
            queue.pop(0)()
            gap -= 0.7
    flush()
    for cp in sent:
        cp.wait_send()


def store(n, *refs):
    sem = refs[-1]
    copies = [pltpu.make_async_copy(refs[i], refs[n + i], sem.at[i]) for i in range(n)]
    for cp in copies:
        cp.start()
    for cp in copies:
        cp.wait()


def on_device(n, nv, queries, keys, values, out_grad, fast_init, updates):
    _, groups, tokens, _, hd = queries.shape
    scale = float(tokens * n) ** (-0.5)
    sr = hd // n
    parent = tree(n)
    edges = len(parent)
    flat = lambda x: x.reshape(groups, tokens, hd)
    hbm = pl.BlockSpec(memory_space=pltpu.HBM)
    vspec = pl.BlockSpec(memory_space=pltpu.VMEM)
    dma = pltpu.SemaphoreType.DMA
    tok_shape = jax.ShapeDtypeStruct((groups, tokens, hd), BF16)
    dq, dk, dv, ig = pl.pallas_call(
        functools.partial(kernel, n, nv, scale, parent),
        out_shape=(tok_shape, tok_shape, tok_shape, jax.ShapeDtypeStruct((3, hd, hd), F32)),
        in_specs=[hbm] * 6,
        out_specs=[vspec] * 4,
        scratch_shapes=[
            pltpu.VMEM((groups, tokens, hd), BF16),
            pltpu.VMEM((groups, tokens, hd), BF16),
            pltpu.VMEM((groups, tokens, hd), BF16),
            pltpu.VMEM((groups, tokens, hd), BF16),
            pltpu.VMEM((3, hd, hd), BF16),
            pltpu.VMEM((2, 3, hd, hd), BF16),
            pltpu.VMEM((3, 3, 2, hd, hd), BF16),
            pltpu.VMEM((3, 2, hd, hd), BF16),
            pltpu.VMEM((2, 3, hd, hd), F32),
            pltpu.VMEM((3, 3, hd, hd), F32),
            pltpu.VMEM((2, 4, 3, sr, hd), F32),
            pltpu.VMEM((3, sr, hd), F32),
            pltpu.VMEM((13, tokens, hd), F32),
            pltpu.VMEM((hd, tokens), BF16),
            pltpu.VMEM((3, edges, 3, sr, hd), F32),
            pltpu.VMEM((nv, 3, sr, hd), F32),
            dma((13,)),
            dma((3, edges, 3)), dma((3, edges, 3)),
            dma((3, edges, 3)), dma((3, edges, 3)),
            dma((nv, 3)), dma((nv, 3)),
        ],
        compiler_params=pltpu.CompilerParams(
            collective_id=0, has_side_effects=True, vmem_limit_bytes=48 * 1024 * 1024
        ),
    )(
        *(
            pltpu.with_memory_space_constraint(x, pltpu.HBM)
            for x in (
                flat(queries), flat(keys), flat(values), flat(out_grad),
                fast_init.reshape(3, hd, hd), updates.reshape(groups - 1, 3, hd, hd),
            )
        ),
    )
    outs = (dq, dk, dv, ig)
    dq, dk, dv, ig = pl.pallas_call(
        functools.partial(store, len(outs)),
        out_shape=tuple(jax.ShapeDtypeStruct(x.shape, x.dtype) for x in outs),
        in_specs=[vspec] * len(outs),
        out_specs=[hbm] * len(outs),
        scratch_shapes=[dma((len(outs),))],
        compiler_params=pltpu.CompilerParams(vmem_limit_bytes=4 * 1024 * 1024),
    )(*outs)
    shaped = lambda x: x.reshape(queries.shape)
    return shaped(dq), shaped(dk), shaped(dv), ig.reshape(fast_init.shape)


def solution(mesh):
    return jax.shard_map(
        functools.partial(on_device, mesh.shape["tok"], mesh.shape["vid"]),
        mesh=mesh,
        in_specs=(
            P("vid", None, "tok", "head", None),
            P("vid", None, "tok", "head", None),
            P("vid", None, "tok", "head", None),
            P("vid", None, "tok", "head", None),
            P("head", None, None, None),
            P("vid", None, "head", None, None, None),
        ),
        out_specs=(
            P("vid", None, "tok", "head", None),
            P("vid", None, "tok", "head", None),
            P("vid", None, "tok", "head", None),
            P("head", None, None, None),
        ),
        check_vma=False,
    )
```

```python
import functools

import jax
import jax.numpy as jnp
from jax import lax
from jax.experimental import pallas as pl
from jax.experimental.pallas import tpu as pltpu
from jax.sharding import PartitionSpec as P

EPS = 1e-06
F32 = jnp.float32
BF16 = jnp.bfloat16
TREES = (
    {1: 0, 3: 0, 2: 1, 4: 3, 6: 3, 5: 4, 7: 6, 8: 6},
    {1: 0, 2: 0, 3: 2, 4: 2, 5: 4, 6: 4, 7: 6, 8: 6},
)
FIXED, HOP = 4.5, 0.4
STAGGER = 1.5


def tree(n, core):
    half = n // 2
    if half == 8:
        up = dict(TREES[core])
    else:
        up = {d: d - 1 for d in range(1, half + 1)}
    parent = dict(up)
    for d, to in up.items():
        if d < n - half:
            parent[-d] = -to
    return parent


def depth(parent):
    t = {0: 0.0}
    for d in sorted(parent, key=lambda d: (abs(d), d)):
        chain = [d]
        while chain[-1] not in t:
            chain.append(parent[chain[-1]])
        for a, b in zip(chain[-2::-1], chain[:0:-1]):
            t[a] = t[b] + FIXED + HOP * abs(a - b)
    return t


def nn(a, b):
    return lax.dot_general(a, b, (((1,), (0,)), ((), ())), preferred_element_type=F32)


def nt(a, b):
    return lax.dot_general(a, b, (((1,), (1,)), ((), ())), preferred_element_type=F32)


def split(x):
    hi = x.astype(BF16)
    return hi, (x - hi.astype(F32)).astype(BF16)


def kernel(n, nv, scale, *refs):
    which = lax.rem(lax.axis_index("head"), 2)
    for core in range(2):
        pl.when(which == core)(functools.partial(body, n, nv, scale, core, *refs))


def body(
    n, nv, scale, core,
    q_h, k_h, v_h, o_h, init_h, upd_h,
    dq_r, dk_r, dv_r, ig_r,
    qv, kv, vv, ov, iv, uv,
    wb, ub, ut, mb, sv, pu, act, tt, rb, vb,
    in_sem, rs_ss, rs_rs, ag_ss, ag_rs, v_ss, v_rs,
):
    hd = iv.shape[1]
    sr = hd // n
    parent = tree(n, core)
    index = {d: i for i, d in enumerate(parent)}
    kids = {d: sorted((e for e in parent if parent[e] == d), key=lambda e: -abs(e)) for d in [0] + list(parent)}
    when = depth(parent)
    span = max(when.values())

    me = lax.axis_index("tok")
    vid = lax.axis_index("vid")
    flip = lambda i: lax.rem(n - i, n) if core else i
    p = flip(me)
    jumps = sorted({(d - parent[d]) % n for d in parent} | {(parent[d] - d) % n for d in parent})
    device = {j: flip(lax.rem(p + j, n)) for j in jumps}

    barrier = pltpu.get_barrier_semaphore()
    for j in jumps:
        pl.semaphore_signal(barrier, inc=1, device_id={"tok": device[j]}, device_id_type=pl.DeviceIdType.MESH)
    for d in range(1, nv):
        pl.semaphore_signal(
            barrier, inc=1, device_id={"vid": lax.rem(vid + d, nv)}, device_id_type=pl.DeviceIdType.MESH
        )

    loads = {}

    def load(name, src, dst, i):
        loads[name] = pltpu.make_async_copy(src, dst, in_sem.at[i])
        loads[name].start()

    load("init", init_h, iv, 0)
    load("upd0", upd_h.at[0], uv.at[0], 1)
    load("upd1", upd_h.at[1], uv.at[1], 2)
    load("q2", q_h.at[2], qv.at[2], 3)
    load("o2", o_h.at[2], ov.at[2], 4)
    load("k1", k_h.at[1], kv.at[1], 5)
    load("v1", v_h.at[1], vv.at[1], 6)
    load("q1", q_h.at[1], qv.at[1], 7)
    load("o1", o_h.at[1], ov.at[1], 8)
    load("k0", k_h.at[0], kv.at[0], 9)
    load("v0", v_h.at[0], vv.at[0], 10)
    load("q0", q_h.at[0], qv.at[0], 11)
    load("o0", o_h.at[0], ov.at[0], 12)

    def rows(shard):
        return pl.ds(pl.multiple_of(lax.rem(shard + 2 * n, n) * sr, 8), sr)

    def weights(m):
        w = iv[m].astype(F32)
        for c in range(3):
            hi, lo = split(w)
            wb[c, m, 0] = hi
            wb[c, m, 1] = lo
            if c < 2:
                up = w + uv[c, m].astype(F32)
                old = jnp.sqrt(jnp.sum(w * w, axis=0, keepdims=True) + EPS)
                new = jnp.sqrt(jnp.sum(up * up, axis=0, keepdims=True) + EPS)
                w = up * (old / new)

    def xw(x, c, m):
        return nn(x, wb[c, m, 0]) + nn(x, wb[c, m, 1])

    def xwt(x, c, m):
        return nt(x, wb[c, m, 0]) + nt(x, wb[c, m, 1])

    def ywt(y, c, m):
        hi, lo = split(y)
        return nt(hi, wb[c, m, 0]) + nt(hi, wb[c, m, 1]) + nt(lo, wb[c, m, 0])

    def yw(y, c, m):
        hi, lo = split(y)
        return nn(hi, wb[c, m, 0]) + nn(hi, wb[c, m, 1]) + nn(lo, wb[c, m, 0])

    def left2(y, x):
        hi, lo = split(y)
        return nn(hi, x) + nn(lo, x)

    def right2(x, y):
        hi, lo = split(y)
        return nn(x, hi) + nn(x, lo)

    def t16(x):
        return x.astype(F32).T.astype(BF16)

    def query_a(c):
        loads[f"q{c}"].wait()
        g = xw(qv[c], c, 0)
        u = xw(qv[c], c, 1)
        s = jax.nn.sigmoid(g)
        a = g * s
        act[0] = u * (s * (1.0 + g * (1.0 - s)))
        act[1] = a
        act[2] = a * u

    def query_d(c):
        dh = xwt(ov[c], c, 2)
        act[0] = dh * act[0]
        act[1] = dh * act[1]

    def query_sum(c, m):
        if m == 2:
            loads[f"o{c}"].wait()
            mb[c, 2] = right2(t16(ov[c]), act[2]) if c else left2(act[2].T, ov[c])
        else:
            mb[c, m] = left2(act[m].T, qv[c]) if c else right2(t16(qv[c]), act[m])

    def query_c(c):
        dq_r[c] = (ywt(act[0], c, 0) + ywt(act[1], c, 1)).astype(BF16)

    def update_a(c):
        loads[f"k{c}"].wait()
        loads[f"v{c}"].wait()
        g = xw(kv[c], c, 0)
        u = xw(kv[c], c, 1)
        b = xwt(vv[c], c, 2)
        s = jax.nn.sigmoid(g)
        a = g * s * scale
        d1 = (s * (1.0 + g * (1.0 - s))) * scale
        d2 = (s * (1.0 - s) * (2.0 + g * (1.0 - 2.0 * s))) * scale
        act[3] = b * u * d2
        act[4] = b * d1
        act[5] = u * d1
        act[6] = a
        act[7] = b * u * d1
        act[8] = b * a
        act[9] = a * u

    def update_t(c):
        if c > 0:
            tt[...] = t16(vv[c])
        else:
            tt[...] = t16(kv[c])

    def kut(c, m):
        return nt(kv[c], ub[m, 0]) + nt(kv[c], ub[m, 1])

    def halves(c, m):
        hi, lo = split(ut[c, m])
        ub[m, 0] = hi
        ub[m, 1] = lo

    def after_gate(c):
        halves(c, 0)
        act[10] = kut(c, 0)

    def after_up(c):
        halves(c, 1)
        act[11] = kut(c, 1)

    def after_down(c):
        halves(c, 2)
        act[12] = nn(vv[c], ub[2, 0]) + nn(vv[c], ub[2, 1])

    def sum_gate(c):
        y = act[10] * act[3] + act[11] * act[4] + act[12] * act[5]
        act[0] = y
        mb[c, 0] += left2(y.T, kv[c]) if c else right2(tt[...], y)

    def sum_up(c):
        y = act[10] * act[4] + act[12] * act[6]
        act[1] = y
        mb[c, 1] += left2(y.T, kv[c]) if c else right2(tt[...], y)

    def sum_down(c):
        y = act[10] * act[5] + act[11] * act[6]
        act[2] = y
        mb[c, 2] += right2(tt[...], y) if c else left2(y.T, vv[c])

    def dot3(y, m, transposed):
        hi, lo = split(y)
        f = nt if transposed else nn
        return f(hi, ub[m, 0]) + f(hi, ub[m, 1]) + f(lo, ub[m, 0])

    def grads_a(c):
        dk_r[c] = (
            dot3(act[7], 0, False) + dot3(act[8], 1, False) + ywt(act[0], c, 0) + ywt(act[1], c, 1)
        ).astype(BF16)

    def grads_b(c):
        dv_r[c] = (dot3(act[9], 2, True) + yw(act[2], c, 2)).astype(BF16)

    def shard_rows():
        at = lax.broadcasted_iota(jnp.int32, (sr, hd), 1) - lax.broadcasted_iota(jnp.int32, (sr, hd), 0)
        pick = jnp.where(at == p * sr, 1.0, 0.0).astype(BF16)
        for m in range(3):
            w = nt(pick, iv[m])
            for c in range(2):
                up = w + nt(pick, uv[c, m])
                old = jnp.sqrt(jnp.sum(w * w, axis=1, keepdims=True) + EPS)
                new = jnp.sqrt(jnp.sum(up * up, axis=1, keepdims=True) + EPS)
                ratio = old / new
                sv[c, 0, m] = up
                sv[c, 1, m] = jnp.broadcast_to(ratio, up.shape)
                sv[c, 2, m] = up * (ratio / (new * new))
                sv[c, 3, m] = w / (old * new)
                w = up * ratio

    def place():
        at = lax.broadcasted_iota(jnp.int32, (sr, hd), 1) - lax.broadcasted_iota(jnp.int32, (sr, hd), 0)
        pick = jnp.where(at == p * sr, 1.0, 0.0)
        for m in range(3):
            mb[0, m] += lax.dot_general(
                pu[m], pick, (((0,), (0,)), ((), ())),
                precision=lax.Precision.HIGHEST, preferred_element_type=F32,
            )

    def copy_to(axis, index, src, dst, ss, rs):
        return pltpu.make_async_remote_copy(
            src_ref=src, dst_ref=dst, send_sem=ss, recv_sem=rs,
            device_id={axis: index}, device_id_type=pl.DeviceIdType.MESH,
        )

    sent = []

    def arrived(at, sem):
        copy_to("tok", device[jumps[0]], at, at, sem, sem).wait_recv()

    def collect(c, m, d):
        own = mb.at[c, m, rows(p - d)]
        if not kids[d]:
            return own
        total = None
        for e in kids[d]:
            at = rb.at[c, index[e], m]
            arrived(at, rs_rs.at[c, index[e], m])
            total = (own[...] if total is None else total) + at[...]
        if d == 0:
            return total
        at = rb.at[c, index[kids[d][0]], m]
        at[...] = total
        return at

    def reduce_send(c, m, d):
        i = index[d]
        cp = copy_to(
            "tok", device[(parent[d] - d) % n], collect(c, m, d), rb.at[c, i, m], rs_ss.at[c, i, m], rs_rs.at[c, i, m]
        )
        cp.start()
        sent.append(cp)

    def gather_send(c, buf, m, d):
        at = buf.at[m, rows(p - d)]
        for e in kids[d]:
            cp = copy_to(
                "tok", device[(e - d) % n], at, at, ag_ss.at[c, index[e], m], ag_rs.at[c, index[e], m]
            )
            cp.start()
            sent.append(cp)

    def gather_step(c, buf, m, d):
        arrived(buf.at[m, rows(p - d)], ag_rs.at[c, index[d], m])
        gather_send(c, buf, m, d)

    def norm_back(c, m, first):
        total = collect(c + 1, m, 0)
        if not first:
            total = total + pu[m]
        inner = jnp.sum(total * sv[c, 0, m], axis=1, keepdims=True)
        step = total * sv[c, 1, m] - inner * sv[c, 2, m]
        ut[c, m, rows(p)] = step
        gather_send(c + 1, ut.at[c], m, 0)
        pu[m] = step + inner * sv[c, 3, m]

    def to_videos(m):
        at = vb.at[vid, m]
        at[...] = collect(0, m, 0)
        for d in range(1, nv):
            cp = copy_to("vid", lax.rem(vid + d, nv), at, at, v_ss.at[d, m], v_rs.at[d, m])
            cp.start()
            sent.append(cp)

    def from_videos(m):
        for d in range(1, nv):
            arrived(vb.at[lax.rem(vid + nv - d, nv), m], v_rs.at[d, m])
        total = vb[0, m]
        for w in range(1, nv):
            total = total + vb[w, m]
        ig_r[m, rows(p)] = total
        gather_send(0, ig_r, m, 0)

    events = []
    queue = []

    def at(t, f, *args):
        events.append((t, len(events), functools.partial(f, *args)))

    def later(*fs):
        queue.extend(fs)

    def flush():
        while queue:
            queue.pop(0)()

    def exchange(c, starts, finish, extra, buf):
        ends = {}
        for m, t in starts.items():
            for d in parent:
                at(t + span - when[d], reduce_send, c, m, d)
            t += span + 0.2
            at(t, finish, m)
            if extra:
                t += extra
                at(t, from_videos, m)
            for d in parent:
                at(t + 0.2 + when[d], gather_step, c, buf, m, d)
            ends[m] = t + 0.2 + span
        return ends

    done = set()

    def once(f, *args):
        if (f, args) not in done:
            done.add((f, args))
            f(*args)

    def zeros():
        dk_r[2] = jnp.zeros(dk_r.shape[1:], BF16)
        dv_r[2] = jnp.zeros(dv_r.shape[1:], BF16)

    for name in ("init", "upd0", "upd1"):
        loads[name].wait()
    weights(0)
    weights(1)
    query_a(2)
    query_sum(2, 2)
    pl.semaphore_wait(barrier, len(jumps) + nv - 1)

    def first_rest():
        weights(2)
        query_d(2)
        query_sum(2, 0)

    at(0.01, first_rest)
    at(STAGGER - 0.01, query_sum, 2, 1)
    later(
        functools.partial(once, shard_rows), lambda: query_c(2), lambda: update_a(1), lambda: update_t(1),
        lambda: query_a(1), lambda: query_sum(1, 2), lambda: query_d(1), lambda: query_sum(1, 0),
        lambda: query_sum(1, 1), lambda: query_c(1), zeros,
    )
    ends = exchange(
        2, {2: 0.0, 0: STAGGER, 1: 2 * STAGGER},
        lambda m: (once(shard_rows), norm_back(1, m, True)), 0, ut.at[1],
    )
    at(ends[2] + 0.01, lambda: (flush(), after_down(1)))
    at(ends[0] + 0.01, lambda: (after_gate(1), sum_up(1)))
    at(ends[1] + 0.01, lambda: (after_up(1), sum_gate(1)))
    t1 = {1: ends[0] + 0.5, 0: ends[1] + 0.5, 2: ends[1] + 0.5 + STAGGER}
    at(t1[0] + 0.01, lambda: (sum_down(1), later(
        lambda: grads_a(1), lambda: grads_b(1), lambda: update_a(0), lambda: update_t(0),
        lambda: query_a(0), lambda: query_sum(0, 2), lambda: query_d(0), lambda: query_sum(0, 0),
        lambda: query_sum(0, 1), lambda: query_c(0),
    )))
    ends = exchange(1, t1, lambda m: norm_back(0, m, False), 0, ut.at[0])
    at(max(t1.values()) + span + 0.3, later, place)
    at(ends[1] + 0.01, lambda: (flush(), after_up(0)))
    at(ends[0] + 0.01, lambda: (after_gate(0), sum_down(0)))
    at(ends[2] + 0.01, lambda: (after_down(0), sum_up(0)))
    t0 = {2: ends[0] + 0.5, 1: ends[2] + 0.5, 0: ends[2] + 0.5 + STAGGER}
    at(t0[1] + 0.01, lambda: (sum_gate(0), later(lambda: grads_a(0), lambda: grads_b(0))))
    exchange(0, t0, to_videos, FIXED + 2 * HOP, ig_r)

    events.sort(key=lambda e: e[:2])
    for (t, _, f), after in zip(events, events[1:] + [(events[-1][0] + 9.0,)]):
        f()
        gap = after[0] - t
        while queue and gap > 0.45:
            queue.pop(0)()
            gap -= 0.7
    flush()
    for cp in sent:
        cp.wait_send()


def store(n, *refs):
    sem = refs[-1]
    copies = [pltpu.make_async_copy(refs[i], refs[n + i], sem.at[i]) for i in range(n)]
    for cp in copies:
        cp.start()
    for cp in copies:
        cp.wait()


def on_device(n, nv, queries, keys, values, out_grad, fast_init, updates):
    _, groups, tokens, _, hd = queries.shape
    scale = float(tokens * n) ** (-0.5)
    sr = hd // n
    edges = n - 1
    flat = lambda x: x.reshape(groups, tokens, hd)
    hbm = pl.BlockSpec(memory_space=pltpu.HBM)
    vspec = pl.BlockSpec(memory_space=pltpu.VMEM)
    dma = pltpu.SemaphoreType.DMA
    tok_shape = jax.ShapeDtypeStruct((groups, tokens, hd), BF16)
    dq, dk, dv, ig = pl.pallas_call(
        functools.partial(kernel, n, nv, scale),
        out_shape=(tok_shape, tok_shape, tok_shape, jax.ShapeDtypeStruct((3, hd, hd), F32)),
        in_specs=[hbm] * 6,
        out_specs=[vspec] * 4,
        scratch_shapes=[
            pltpu.VMEM((groups, tokens, hd), BF16),
            pltpu.VMEM((groups, tokens, hd), BF16),
            pltpu.VMEM((groups, tokens, hd), BF16),
            pltpu.VMEM((groups, tokens, hd), BF16),
            pltpu.VMEM((3, hd, hd), BF16),
            pltpu.VMEM((2, 3, hd, hd), BF16),
            pltpu.VMEM((3, 3, 2, hd, hd), BF16),
            pltpu.VMEM((3, 2, hd, hd), BF16),
            pltpu.VMEM((2, 3, hd, hd), F32),
            pltpu.VMEM((3, 3, hd, hd), F32),
            pltpu.VMEM((2, 4, 3, sr, hd), F32),
            pltpu.VMEM((3, sr, hd), F32),
            pltpu.VMEM((13, tokens, hd), F32),
            pltpu.VMEM((hd, tokens), BF16),
            pltpu.VMEM((3, edges, 3, sr, hd), F32),
            pltpu.VMEM((nv, 3, sr, hd), F32),
            dma((13,)),
            dma((3, edges, 3)), dma((3, edges, 3)),
            dma((3, edges, 3)), dma((3, edges, 3)),
            dma((nv, 3)), dma((nv, 3)),
        ],
        compiler_params=pltpu.CompilerParams(
            collective_id=0, has_side_effects=True, vmem_limit_bytes=48 * 1024 * 1024
        ),
    )(
        *(
            pltpu.with_memory_space_constraint(x, pltpu.HBM)
            for x in (
                flat(queries), flat(keys), flat(values), flat(out_grad),
                fast_init.reshape(3, hd, hd), updates.reshape(groups - 1, 3, hd, hd),
            )
        ),
    )
    outs = (dq, dk, dv, ig)
    dq, dk, dv, ig = pl.pallas_call(
        functools.partial(store, len(outs)),
        out_shape=tuple(jax.ShapeDtypeStruct(x.shape, x.dtype) for x in outs),
        in_specs=[vspec] * len(outs),
        out_specs=[hbm] * len(outs),
        scratch_shapes=[dma((len(outs),))],
        compiler_params=pltpu.CompilerParams(vmem_limit_bytes=4 * 1024 * 1024),
    )(*outs)
    shaped = lambda x: x.reshape(queries.shape)
    return shaped(dq), shaped(dk), shaped(dv), ig.reshape(fast_init.shape)


def solution(mesh):
    return jax.shard_map(
        functools.partial(on_device, mesh.shape["tok"], mesh.shape["vid"]),
        mesh=mesh,
        in_specs=(
            P("vid", None, "tok", "head", None),
            P("vid", None, "tok", "head", None),
            P("vid", None, "tok", "head", None),
            P("vid", None, "tok", "head", None),
            P("head", None, None, None),
            P("vid", None, "head", None, None, None),
        ),
        out_specs=(
            P("vid", None, "tok", "head", None),
            P("vid", None, "tok", "head", None),
            P("vid", None, "tok", "head", None),
            P("head", None, None, None),
        ),
        check_vma=False,
    )
```

```python
import functools

import jax
import jax.numpy as jnp
from jax import lax
from jax.experimental import pallas as pl
from jax.experimental.pallas import tpu as pltpu
from jax.sharding import PartitionSpec as P

EPS = 1e-06
F32 = jnp.float32
BF16 = jnp.bfloat16
TREES = (
    {1: 0, 3: 0, 2: 1, 4: 3, 6: 3, 5: 4, 7: 6, 8: 6},
    {1: 0, 2: 0, 3: 2, 4: 2, 5: 4, 6: 4, 7: 6, 8: 6},
)
FIXED, HOP = 4.5, 0.4
STAGGER = 1.5


def tree(n, core):
    half = n // 2
    if half == 8:
        up = dict(TREES[core])
    else:
        up = {d: d - 1 for d in range(1, half + 1)}
    parent = dict(up)
    for d, to in up.items():
        if d < n - half:
            parent[-d] = -to
    return parent


def depth(parent):
    t = {0: 0.0}
    for d in sorted(parent, key=lambda d: (abs(d), d)):
        chain = [d]
        while chain[-1] not in t:
            chain.append(parent[chain[-1]])
        for a, b in zip(chain[-2::-1], chain[:0:-1]):
            t[a] = t[b] + FIXED + HOP * abs(a - b)
    return t


def nn(a, b):
    return lax.dot_general(a, b, (((1,), (0,)), ((), ())), preferred_element_type=F32)


def nt(a, b):
    return lax.dot_general(a, b, (((1,), (1,)), ((), ())), preferred_element_type=F32)


def split(x):
    hi = x.astype(BF16)
    return hi, (x - hi.astype(F32)).astype(BF16)


def kernel(n, nv, scale, *refs):
    which = lax.rem(lax.axis_index("head"), 2)
    for core in range(2):
        pl.when(which == core)(functools.partial(body, n, nv, scale, core, *refs))


def body(
    n, nv, scale, core,
    q_h, k_h, v_h, o_h, init_h, upd_h,
    dq_r, dk_r, dv_r, ig_r,
    qv, kv, vv, ov, iv, uv,
    wb, ub, ut, mb, sv, pu, act, tt, rb, vb,
    in_sem, rs_ss, rs_rs, ag_ss, ag_rs, v_ss, v_rs,
):
    hd = iv.shape[1]
    sr = hd // n
    parent = tree(n, core)
    index = {d: i for i, d in enumerate(parent)}
    kids = {d: sorted((e for e in parent if parent[e] == d), key=lambda e: -abs(e)) for d in [0] + list(parent)}
    when = depth(parent)
    span = max(when.values())

    me = lax.axis_index("tok")
    vid = lax.axis_index("vid")
    flip = lambda i: lax.rem(n - i, n) if core else i
    p = flip(me)
    jumps = sorted({(d - parent[d]) % n for d in parent} | {(parent[d] - d) % n for d in parent})
    device = {j: flip(lax.rem(p + j, n)) for j in jumps}

    barrier = pltpu.get_barrier_semaphore()
    for j in jumps:
        pl.semaphore_signal(barrier, inc=1, device_id={"tok": device[j]}, device_id_type=pl.DeviceIdType.MESH)
    for d in range(1, nv):
        pl.semaphore_signal(
            barrier, inc=1, device_id={"vid": lax.rem(vid + d, nv)}, device_id_type=pl.DeviceIdType.MESH
        )

    loads = {}

    def load(name, src, dst, i):
        loads[name] = pltpu.make_async_copy(src, dst, in_sem.at[i])
        loads[name].start()

    load("init", init_h, iv, 0)
    load("upd0", upd_h.at[0], uv.at[0], 1)
    load("upd1", upd_h.at[1], uv.at[1], 2)
    load("q2", q_h.at[2], qv.at[2], 3)
    load("o2", o_h.at[2], ov.at[2], 4)
    load("k1", k_h.at[1], kv.at[1], 5)
    load("v1", v_h.at[1], vv.at[1], 6)
    load("q1", q_h.at[1], qv.at[1], 7)
    load("o1", o_h.at[1], ov.at[1], 8)
    load("k0", k_h.at[0], kv.at[0], 9)
    load("v0", v_h.at[0], vv.at[0], 10)
    load("q0", q_h.at[0], qv.at[0], 11)
    load("o0", o_h.at[0], ov.at[0], 12)

    def rows(shard):
        return pl.ds(pl.multiple_of(lax.rem(shard + 2 * n, n) * sr, 8), sr)

    def weights(m, groups):
        w = iv[m].astype(F32)
        for c in range(max(groups) + 1):
            if c in groups:
                hi, lo = split(w)
                wb[c, m, 0] = hi
                wb[c, m, 1] = lo
            if c < max(groups):
                up = w + uv[c, m].astype(F32)
                old = jnp.sqrt(jnp.sum(w * w, axis=0, keepdims=True) + EPS)
                new = jnp.sqrt(jnp.sum(up * up, axis=0, keepdims=True) + EPS)
                w = up * (old / new)

    def xw(x, c, m):
        return nn(x, wb[c, m, 0]) + nn(x, wb[c, m, 1])

    def xwt(x, c, m):
        return nt(x, wb[c, m, 0]) + nt(x, wb[c, m, 1])

    def ywt(y, c, m):
        hi, lo = split(y)
        return nt(hi, wb[c, m, 0]) + nt(hi, wb[c, m, 1]) + nt(lo, wb[c, m, 0])

    def yw(y, c, m):
        hi, lo = split(y)
        return nn(hi, wb[c, m, 0]) + nn(hi, wb[c, m, 1]) + nn(lo, wb[c, m, 0])

    def left2(y, x):
        hi, lo = split(y)
        return nn(hi, x) + nn(lo, x)

    def right2(x, y):
        hi, lo = split(y)
        return nn(x, hi) + nn(x, lo)

    def t16(x):
        return x.astype(F32).T.astype(BF16)

    def query_a(c):
        loads[f"q{c}"].wait()
        g = xw(qv[c], c, 0)
        u = xw(qv[c], c, 1)
        s = jax.nn.sigmoid(g)
        a = g * s
        act[0] = u * (s * (1.0 + g * (1.0 - s)))
        act[1] = a
        act[2] = a * u

    def query_d(c):
        dh = xwt(ov[c], c, 2)
        act[0] = dh * act[0]
        act[1] = dh * act[1]

    def query_sum(c, m):
        if m == 2:
            loads[f"o{c}"].wait()
            mb[c, 2] = right2(t16(ov[c]), act[2]) if c else left2(act[2].T, ov[c])
        else:
            mb[c, m] = left2(act[m].T, qv[c]) if c else right2(t16(qv[c]), act[m])

    def query_c(c):
        dq_r[c] = (ywt(act[0], c, 0) + ywt(act[1], c, 1)).astype(BF16)

    def update_a(c):
        loads[f"k{c}"].wait()
        loads[f"v{c}"].wait()
        g = xw(kv[c], c, 0)
        u = xw(kv[c], c, 1)
        b = xwt(vv[c], c, 2)
        s = jax.nn.sigmoid(g)
        a = g * s * scale
        d1 = (s * (1.0 + g * (1.0 - s))) * scale
        d2 = (s * (1.0 - s) * (2.0 + g * (1.0 - 2.0 * s))) * scale
        act[3] = b * u * d2
        act[4] = b * d1
        act[5] = u * d1
        act[6] = a
        act[7] = b * u * d1
        act[8] = b * a
        act[9] = a * u

    def update_t(c):
        if c > 0:
            tt[...] = t16(vv[c])
        else:
            tt[...] = t16(kv[c])

    def kut(c, m):
        return nt(kv[c], ub[m, 0]) + nt(kv[c], ub[m, 1])

    def halves(c, m):
        hi, lo = split(ut[c, m])
        ub[m, 0] = hi
        ub[m, 1] = lo

    def after_gate(c):
        halves(c, 0)
        act[10] = kut(c, 0)

    def after_up(c):
        halves(c, 1)
        act[11] = kut(c, 1)

    def after_down(c):
        halves(c, 2)
        act[12] = nn(vv[c], ub[2, 0]) + nn(vv[c], ub[2, 1])

    def sum_gate(c):
        y = act[10] * act[3] + act[11] * act[4] + act[12] * act[5]
        act[0] = y
        mb[c, 0] += left2(y.T, kv[c]) if c else right2(tt[...], y)

    def sum_up(c):
        y = act[10] * act[4] + act[12] * act[6]
        act[1] = y
        mb[c, 1] += left2(y.T, kv[c]) if c else right2(tt[...], y)

    def sum_down(c):
        y = act[10] * act[5] + act[11] * act[6]
        act[2] = y
        mb[c, 2] += right2(tt[...], y) if c else left2(y.T, vv[c])

    def dot3(y, m, transposed):
        hi, lo = split(y)
        f = nt if transposed else nn
        return f(hi, ub[m, 0]) + f(hi, ub[m, 1]) + f(lo, ub[m, 0])

    def grads_a(c):
        dk_r[c] = (
            dot3(act[7], 0, False) + dot3(act[8], 1, False) + ywt(act[0], c, 0) + ywt(act[1], c, 1)
        ).astype(BF16)

    def grads_b(c):
        dv_r[c] = (dot3(act[9], 2, True) + yw(act[2], c, 2)).astype(BF16)

    def shard_rows():
        at = lax.broadcasted_iota(jnp.int32, (sr, hd), 1) - lax.broadcasted_iota(jnp.int32, (sr, hd), 0)
        pick = jnp.where(at == p * sr, 1.0, 0.0).astype(BF16)
        for m in range(3):
            w = nt(pick, iv[m])
            for c in range(2):
                up = w + nt(pick, uv[c, m])
                old = jnp.sqrt(jnp.sum(w * w, axis=1, keepdims=True) + EPS)
                new = jnp.sqrt(jnp.sum(up * up, axis=1, keepdims=True) + EPS)
                ratio = old / new
                sv[c, 0, m] = up
                sv[c, 1, m] = jnp.broadcast_to(ratio, up.shape)
                sv[c, 2, m] = up * (ratio / (new * new))
                sv[c, 3, m] = w / (old * new)
                w = up * ratio

    def place():
        at = lax.broadcasted_iota(jnp.int32, (sr, hd), 1) - lax.broadcasted_iota(jnp.int32, (sr, hd), 0)
        pick = jnp.where(at == p * sr, 1.0, 0.0)
        for m in range(3):
            mb[0, m] += lax.dot_general(
                pu[m], pick, (((0,), (0,)), ((), ())),
                precision=lax.Precision.HIGHEST, preferred_element_type=F32,
            )

    def copy_to(axis, index, src, dst, ss, rs):
        return pltpu.make_async_remote_copy(
            src_ref=src, dst_ref=dst, send_sem=ss, recv_sem=rs,
            device_id={axis: index}, device_id_type=pl.DeviceIdType.MESH,
        )

    sent = []

    def arrived(at, sem):
        copy_to("tok", device[jumps[0]], at, at, sem, sem).wait_recv()

    def collect(c, m, d):
        own = mb.at[c, m, rows(p - d)]
        if not kids[d]:
            return own
        total = None
        for e in kids[d]:
            at = rb.at[c, index[e], m]
            arrived(at, rs_rs.at[c, index[e], m])
            total = (own[...] if total is None else total) + at[...]
        if d == 0:
            return total
        at = rb.at[c, index[kids[d][0]], m]
        at[...] = total
        return at

    def reduce_send(c, m, d):
        i = index[d]
        cp = copy_to(
            "tok", device[(parent[d] - d) % n], collect(c, m, d), rb.at[c, i, m], rs_ss.at[c, i, m], rs_rs.at[c, i, m]
        )
        cp.start()
        sent.append(cp)

    def gather_send(c, buf, m, d):
        at = buf.at[m, rows(p - d)]
        for e in kids[d]:
            cp = copy_to(
                "tok", device[(e - d) % n], at, at, ag_ss.at[c, index[e], m], ag_rs.at[c, index[e], m]
            )
            cp.start()
            sent.append(cp)

    def gather_step(c, buf, m, d):
        arrived(buf.at[m, rows(p - d)], ag_rs.at[c, index[d], m])
        gather_send(c, buf, m, d)

    def norm_back(c, m, first):
        total = collect(c + 1, m, 0)
        if not first:
            total = total + pu[m]
        inner = jnp.sum(total * sv[c, 0, m], axis=1, keepdims=True)
        step = total * sv[c, 1, m] - inner * sv[c, 2, m]
        ut[c, m, rows(p)] = step
        gather_send(c + 1, ut.at[c], m, 0)
        pu[m] = step + inner * sv[c, 3, m]

    def to_videos(m):
        at = vb.at[vid, m]
        at[...] = collect(0, m, 0)
        for d in range(1, nv):
            cp = copy_to("vid", lax.rem(vid + d, nv), at, at, v_ss.at[d, m], v_rs.at[d, m])
            cp.start()
            sent.append(cp)

    def from_videos(m):
        for d in range(1, nv):
            arrived(vb.at[lax.rem(vid + nv - d, nv), m], v_rs.at[d, m])
        total = vb[0, m]
        for w in range(1, nv):
            total = total + vb[w, m]
        ig_r[m, rows(p)] = total
        gather_send(0, ig_r, m, 0)

    events = []
    queue = []

    def at(t, f, *args):
        events.append((t, len(events), functools.partial(f, *args)))

    def later(*fs):
        queue.extend(fs)

    def flush():
        while queue:
            queue.pop(0)()

    def exchange(c, starts, finish, extra, buf):
        ends = {}
        for m, t in starts.items():
            for d in parent:
                at(t + span - when[d], reduce_send, c, m, d)
            t += span + 0.2
            at(t, finish, m)
            if extra:
                t += extra
                at(t, from_videos, m)
            for d in parent:
                at(t + 0.2 + when[d], gather_step, c, buf, m, d)
            ends[m] = t + 0.2 + span
        return ends

    done = set()

    def once(f, *args):
        if (f, args) not in done:
            done.add((f, args))
            f(*args)

    def zeros():
        dk_r[2] = jnp.zeros(dk_r.shape[1:], BF16)
        dv_r[2] = jnp.zeros(dv_r.shape[1:], BF16)

    for name in ("init", "upd0", "upd1"):
        loads[name].wait()
    weights(0, (2,))
    weights(1, (2,))
    query_a(2)
    query_sum(2, 2)
    pl.semaphore_wait(barrier, len(jumps) + nv - 1)

    def first_rest():
        weights(2, (2,))
        query_d(2)
        query_sum(2, 0)

    at(0.01, first_rest)
    at(STAGGER - 0.01, query_sum, 2, 1)
    later(
        functools.partial(once, shard_rows), lambda: query_c(2), lambda: weights(0, (0, 1)), lambda: weights(1, (0, 1)),
        lambda: weights(2, (0, 1)), lambda: update_a(1), lambda: update_t(1),
        lambda: query_a(1), lambda: query_sum(1, 2), lambda: query_d(1), lambda: query_sum(1, 0),
        lambda: query_sum(1, 1), lambda: query_c(1), zeros,
    )
    ends = exchange(
        2, {2: 0.0, 0: STAGGER, 1: 2 * STAGGER},
        lambda m: (once(shard_rows), norm_back(1, m, True)), 0, ut.at[1],
    )
    at(ends[2] + 0.01, lambda: (flush(), after_down(1)))
    at(ends[0] + 0.01, lambda: (after_gate(1), sum_up(1)))
    at(ends[1] + 0.01, lambda: (after_up(1), sum_gate(1)))
    t1 = {1: ends[0] + 0.5, 0: ends[1] + 0.5, 2: ends[1] + 0.5 + STAGGER}
    at(t1[0] + 0.01, lambda: (sum_down(1), later(
        lambda: grads_a(1), lambda: grads_b(1), lambda: update_a(0), lambda: update_t(0),
        lambda: query_a(0), lambda: query_sum(0, 2), lambda: query_d(0), lambda: query_sum(0, 0),
        lambda: query_sum(0, 1), lambda: query_c(0),
    )))
    ends = exchange(1, t1, lambda m: norm_back(0, m, False), 0, ut.at[0])
    at(max(t1.values()) + span + 0.3, later, place)
    at(ends[1] + 0.01, lambda: (flush(), after_up(0)))
    at(ends[0] + 0.01, lambda: (after_gate(0), sum_down(0)))
    at(ends[2] + 0.01, lambda: (after_down(0), sum_up(0)))
    t0 = {2: ends[0] + 0.5, 1: ends[2] + 0.5, 0: ends[2] + 0.5 + STAGGER}
    at(t0[1] + 0.01, lambda: (sum_gate(0), later(lambda: grads_a(0), lambda: grads_b(0))))
    exchange(0, t0, to_videos, FIXED + 2 * HOP, ig_r)

    events.sort(key=lambda e: e[:2])
    for (t, _, f), after in zip(events, events[1:] + [(events[-1][0] + 9.0,)]):
        f()
        gap = after[0] - t
        while queue and gap > 0.45:
            queue.pop(0)()
            gap -= 0.7
    flush()
    for cp in sent:
        cp.wait_send()


def store(n, *refs):
    sem = refs[-1]
    copies = [pltpu.make_async_copy(refs[i], refs[n + i], sem.at[i]) for i in range(n)]
    for cp in copies:
        cp.start()
    for cp in copies:
        cp.wait()


def on_device(n, nv, queries, keys, values, out_grad, fast_init, updates):
    _, groups, tokens, _, hd = queries.shape
    scale = float(tokens * n) ** (-0.5)
    sr = hd // n
    edges = n - 1
    flat = lambda x: x.reshape(groups, tokens, hd)
    hbm = pl.BlockSpec(memory_space=pltpu.HBM)
    vspec = pl.BlockSpec(memory_space=pltpu.VMEM)
    dma = pltpu.SemaphoreType.DMA
    tok_shape = jax.ShapeDtypeStruct((groups, tokens, hd), BF16)
    dq, dk, dv, ig = pl.pallas_call(
        functools.partial(kernel, n, nv, scale),
        out_shape=(tok_shape, tok_shape, tok_shape, jax.ShapeDtypeStruct((3, hd, hd), F32)),
        in_specs=[hbm] * 6,
        out_specs=[vspec] * 4,
        scratch_shapes=[
            pltpu.VMEM((groups, tokens, hd), BF16),
            pltpu.VMEM((groups, tokens, hd), BF16),
            pltpu.VMEM((groups, tokens, hd), BF16),
            pltpu.VMEM((groups, tokens, hd), BF16),
            pltpu.VMEM((3, hd, hd), BF16),
            pltpu.VMEM((2, 3, hd, hd), BF16),
            pltpu.VMEM((3, 3, 2, hd, hd), BF16),
            pltpu.VMEM((3, 2, hd, hd), BF16),
            pltpu.VMEM((2, 3, hd, hd), F32),
            pltpu.VMEM((3, 3, hd, hd), F32),
            pltpu.VMEM((2, 4, 3, sr, hd), F32),
            pltpu.VMEM((3, sr, hd), F32),
            pltpu.VMEM((13, tokens, hd), F32),
            pltpu.VMEM((hd, tokens), BF16),
            pltpu.VMEM((3, edges, 3, sr, hd), F32),
            pltpu.VMEM((nv, 3, sr, hd), F32),
            dma((13,)),
            dma((3, edges, 3)), dma((3, edges, 3)),
            dma((3, edges, 3)), dma((3, edges, 3)),
            dma((nv, 3)), dma((nv, 3)),
        ],
        compiler_params=pltpu.CompilerParams(
            collective_id=0, has_side_effects=True, vmem_limit_bytes=48 * 1024 * 1024
        ),
    )(
        *(
            pltpu.with_memory_space_constraint(x, pltpu.HBM)
            for x in (
                flat(queries), flat(keys), flat(values), flat(out_grad),
                fast_init.reshape(3, hd, hd), updates.reshape(groups - 1, 3, hd, hd),
            )
        ),
    )
    outs = (dq, dk, dv, ig)
    dq, dk, dv, ig = pl.pallas_call(
        functools.partial(store, len(outs)),
        out_shape=tuple(jax.ShapeDtypeStruct(x.shape, x.dtype) for x in outs),
        in_specs=[vspec] * len(outs),
        out_specs=[hbm] * len(outs),
        scratch_shapes=[dma((len(outs),))],
        compiler_params=pltpu.CompilerParams(vmem_limit_bytes=4 * 1024 * 1024),
    )(*outs)
    shaped = lambda x: x.reshape(queries.shape)
    return shaped(dq), shaped(dk), shaped(dv), ig.reshape(fast_init.shape)


def solution(mesh):
    return jax.shard_map(
        functools.partial(on_device, mesh.shape["tok"], mesh.shape["vid"]),
        mesh=mesh,
        in_specs=(
            P("vid", None, "tok", "head", None),
            P("vid", None, "tok", "head", None),
            P("vid", None, "tok", "head", None),
            P("vid", None, "tok", "head", None),
            P("head", None, None, None),
            P("vid", None, "head", None, None, None),
        ),
        out_specs=(
            P("vid", None, "tok", "head", None),
            P("vid", None, "tok", "head", None),
            P("vid", None, "tok", "head", None),
            P("head", None, None, None),
        ),
        check_vma=False,
    )
```
